512 devices in a mesh: src: 16 (over z, core), row: 32 (over x, y).
Axes of the slice: x: 4, y: 8, z: 8, core: 2. Of those that a mesh axis runs over, the one named last changes fastest.
Arguments:
- spec_re: bfloat16 [1024, 1024], P('row'), may hold values from -18 to 18
- spec_im: bfloat16 [1024, 1024], P('row'), may hold values from -18 to 18
- target: float32 [1024, 1024], P('row'), may hold values from 0.3 to 1.5
- weights: float32 [128], P('src'), may hold values from 0.25 to 2.5
- cent_row: int32 [128], P('src'), may hold values from 128 to 895
- cent_col: int32 [128], P('src'), may hold values from 128 to 895
Outputs:
- grad_re: float32 [1024, 1024], P('row')
- grad_im: float32 [1024, 1024], P('row')
The draws below stay inside these ranges and needn't reach their ends.
Inputs may be any that keep to these rules, and one draw needn't show every extreme that they name: Every pupil disk of radius 128 about (cent_row, cent_col) lies inside the band.
All inputs are finite; a program needn't handle non-finite values.
Results may differ from the reference program's by a relative error of at most 0.0072.
Values may be sent and summed in bfloat16 or wider, within the bound.
No kernel may reach another device: no remote copies, remote signals or barrier semaphores. Data moves between devices by JAX's collectives and lax.ppermute only.
A program may use at most 128 MiB of HBM per device.

```python
import math
import jax
import jax.numpy as jnp
from jax import lax

BAND = 1024
RAD = 128
POINTS = 128


def with_ends(drawn, key, least, high):
    dims = drawn.shape
    place = [jax.random.randint(jax.random.fold_in(key, axis), (), 0, dims[axis]) for axis in range(len(dims))]
    drawn = drawn.at[tuple(place)].set(least)
    longest = dims.index(max(dims))
    place[longest] = (place[longest] + 1) % dims[longest]
    return drawn.at[tuple(place)].set(high)


def levels(stream_key, dims, pieces, least, high):
    level = 1.0
    for dim, shards_of in pieces:
        steps = jax.random.uniform(jax.random.fold_in(jax.random.fold_in(stream_key, 6), dim), (shards_of,), jnp.float32, least / len(pieces), high / len(pieces))
        level = level * jnp.repeat(jnp.exp(steps), dims[dim] // shards_of).reshape((-1,) + (1,) * (len(dims) - 1 - dim))
    return level


def normal_values(own_key, shape, deviation, limit, cuts=(), kind=jnp.bfloat16):
    level = levels(own_key, shape, cuts, -0.22, 0.18) if cuts else 1.0
    result = jax.random.normal(own_key, shape, jnp.float32) * deviation * level
    return jnp.minimum(jnp.maximum(result, -limit), limit).astype(kind)


def setup_inputs(seed: int = 0) -> dict:
    keys = jax.random.split(jax.random.key(seed), 7)
    spec_re = normal_values(keys[0], (BAND, BAND), 3.0, 18.0, ((0, 32),))
    spec_im = normal_values(keys[1], (BAND, BAND), 3.0, 18.0, ((0, 32),))
    target = jnp.clip(0.3 + 1.2 * jax.random.uniform(keys[2], (BAND, BAND), jnp.float32) ** levels(keys[2], (BAND, BAND), ((0, 32),), -0.2, 0.2), 0.3, 1.5)
    weights = jnp.clip(jnp.exp(math.log(2.5) - 2.3025851 * jax.random.uniform(keys[3], (POINTS,), jnp.float32) ** levels(keys[3], (POINTS,), ((0, 16),), -0.2, 0.2)), 0.25, 2.5)
    cent_row = with_ends(jax.random.randint(keys[4], (POINTS,), RAD, BAND - RAD), jax.random.fold_in(keys[4], 1), RAD, (BAND - RAD) - 1).astype(jnp.int32)
    cent_col = with_ends(jax.random.randint(keys[5], (POINTS,), RAD, BAND - RAD), jax.random.fold_in(keys[5], 1), RAD, (BAND - RAD) - 1).astype(jnp.int32)
    return {"spec_re": spec_re, "spec_im": spec_im, "target": target, "weights": weights, "cent_row": cent_row, "cent_col": cent_col}


def make_tables(band):
    position = jnp.arange(band, dtype=jnp.int32)
    phase = position[:, None] * position[None, :] % band
    angle = phase.astype(jnp.float32) * (2.0 * math.pi / band)
    factor = 1.0 / math.sqrt(band)
    return ((jnp.cos(angle) * factor).astype(jnp.bfloat16), (jnp.sin(angle) * factor).astype(jnp.bfloat16))

def reference(spec_re, spec_im, target, weights, cent_row, cent_col):
    band = spec_re.shape[0]
    window = 2 * RAD + 1
    cosine, sine = make_tables(band)
    offsets = jnp.arange(window, dtype=jnp.int32) - RAD
    inside_disk = offsets[:, None] ** 2 + offsets[None, :] ** 2 <= RAD * RAD
    zero_value = jnp.zeros((), jnp.bfloat16)

    def point_field(point):
        first_row = (cent_row[point] - RAD).astype(jnp.int32)
        first_col = (cent_col[point] - RAD).astype(jnp.int32)
        masked_re = jnp.where(inside_disk, lax.dynamic_slice(spec_re, (first_row, first_col), (window, window)), zero_value)
        masked_im = jnp.where(inside_disk, lax.dynamic_slice(spec_im, (first_row, first_col), (window, window)), zero_value)
        cos_col = lax.dynamic_slice_in_dim(cosine, first_col, window, 0)
        sin_col = lax.dynamic_slice_in_dim(sine, first_col, window, 0)
        cos_row = lax.dynamic_slice_in_dim(cosine, first_row, window, 0)
        sin_row = lax.dynamic_slice_in_dim(sine, first_row, window, 0)
        col_re = (jnp.dot(masked_re, cos_col, preferred_element_type=jnp.float32) - jnp.dot(masked_im, sin_col, preferred_element_type=jnp.float32)).astype(jnp.bfloat16)
        col_im = (jnp.dot(masked_re, sin_col, preferred_element_type=jnp.float32) + jnp.dot(masked_im, cos_col, preferred_element_type=jnp.float32)).astype(jnp.bfloat16)
        field_re = jnp.dot(col_re.T, cos_row, preferred_element_type=jnp.float32) - jnp.dot(col_im.T, sin_row, preferred_element_type=jnp.float32)
        field_im = jnp.dot(col_re.T, sin_row, preferred_element_type=jnp.float32) + jnp.dot(col_im.T, cos_row, preferred_element_type=jnp.float32)
        return (field_re, field_im, first_row, first_col, cos_col, sin_col, cos_row, sin_row)

    def add_power(accumulated, point):
        field_re, field_im = point_field(point)[:2]
        return (accumulated + weights[point] * (field_re * field_re + field_im * field_im), None)
    points_all = jnp.arange(POINTS, dtype=jnp.int32)
    power_sum, _ = lax.scan(add_power, jnp.zeros((band, band), jnp.float32), points_all)
    intensity = power_sum / POINTS
    mismatch = intensity - target

    def add_gradient(carry, point):
        total_re, total_im = carry
        field_re, field_im, first_row, first_col, cos_col, sin_col, cos_row, sin_row = point_field(point)
        grad_fre = (2.0 * weights[point] * mismatch * field_re).astype(jnp.bfloat16)
        grad_fim = (2.0 * weights[point] * mismatch * field_im).astype(jnp.bfloat16)
        adj_re = (jnp.dot(grad_fre, cos_row.T, preferred_element_type=jnp.float32) + jnp.dot(grad_fim, sin_row.T, preferred_element_type=jnp.float32)).astype(jnp.bfloat16)
        adj_im = (jnp.dot(grad_fim, cos_row.T, preferred_element_type=jnp.float32) - jnp.dot(grad_fre, sin_row.T, preferred_element_type=jnp.float32)).astype(jnp.bfloat16)
        term_re = jnp.dot(adj_re.T, cos_col.T, preferred_element_type=jnp.float32) + jnp.dot(adj_im.T, sin_col.T, preferred_element_type=jnp.float32)
        term_im = jnp.dot(adj_im.T, cos_col.T, preferred_element_type=jnp.float32) - jnp.dot(adj_re.T, sin_col.T, preferred_element_type=jnp.float32)
        term_re = jnp.where(inside_disk, term_re, jnp.zeros((), jnp.float32))
        term_im = jnp.where(inside_disk, term_im, jnp.zeros((), jnp.float32))
        old_re = lax.dynamic_slice(total_re, (first_row, first_col), (window, window))
        old_im = lax.dynamic_slice(total_im, (first_row, first_col), (window, window))
        total_re = lax.dynamic_update_slice(total_re, old_re + term_re, (first_row, first_col))
        total_im = lax.dynamic_update_slice(total_im, old_im + term_im, (first_row, first_col))
        return ((total_re, total_im), None)
    empty_grid = jnp.zeros((band, band), jnp.float32)
    (grad_re, grad_im), _ = lax.scan(add_gradient, (empty_grid, empty_grid), points_all)
    return (grad_re, grad_im)
```

```python
import functools
import math

import jax
import jax.numpy as jnp
from jax import lax
from jax.experimental import pallas as pl
from jax.experimental.pallas import tpu as pltpu
from jax.sharding import PartitionSpec as P

RAD = 128
F32 = jnp.float32
BF16 = jnp.bfloat16
CHUNK = 256
LANES = 128

WHOLE = pl.BlockSpec(memory_space=pltpu.VMEM)
SCALARS = pl.BlockSpec(memory_space=pltpu.SMEM)


def trig_rows(band):
    index = jnp.arange(32, dtype=jnp.int32)
    rows = jnp.where(index < 16, 64 * index, jnp.where(index < 24, 8 * (index - 16), index - 24))
    phase = rows[:, None] * jnp.arange(band, dtype=jnp.int32)[None, :]
    both = jnp.concatenate([phase, phase + (band - band // 4)], axis=0) % band
    return jnp.cos(both.astype(F32) * (2.0 * math.pi / band))


def inside(first_row, first_col, shape, centre_row, centre_col):
    row_gap = lax.broadcasted_iota(jnp.int32, shape, 0) + (first_row - centre_row)
    col_gap = lax.broadcasted_iota(jnp.int32, shape, 1) + (first_col - centre_col)
    return row_gap * row_gap + col_gap * col_gap <= RAD * RAD


def scatter_blocks(product, out_ref):
    group = lax.broadcasted_iota(jnp.int32, (32, LANES), 1) // 32
    for tile in range(CHUNK // LANES):
        for quad in range(4):
            rows = [
                product[32 * (4 * quad + j) : 32 * (4 * quad + j) + 32, tile * LANES : (tile + 1) * LANES]
                for j in range(4)
            ]
            for dest in range(4):
                joined = None
                for j in range(4):
                    shift = (32 * (j - dest)) % LANES
                    moved = pltpu.roll(rows[j], shift, 1) if shift else rows[j]
                    joined = moved if joined is None else jnp.where(group == j, moved, joined)
                out_ref[4 * tile + dest, :, quad * LANES : (quad + 1) * LANES] = joined.astype(BF16)


def spectrum_kernel(row_ref, cr_ref, cc_ref, trig_ref, re_ref, im_ref, cos_ref, sin_ref, out_ref, lhs_ref):
    step = pl.program_id(0)
    rows, band = re_ref.shape
    points = cr_ref.shape[0]
    half = rows * points

    @pl.when(step == 0)
    def _():
        spec_re = re_ref[...].astype(F32)
        spec_im = im_ref[...].astype(F32)
        for p in range(points):
            keep = inside(row_ref[0] * rows, 0, (rows, band), cr_ref[p], cc_ref[p])
            part_re = jnp.where(keep, spec_re, 0.0)
            part_im = jnp.where(keep, spec_im, 0.0)
            top = slice(p * rows, (p + 1) * rows)
            low = slice(half + p * rows, half + (p + 1) * rows)
            lhs_ref[top, :band] = part_re.astype(BF16)
            lhs_ref[low, band:] = part_re.astype(BF16)
            lhs_ref[low, :band] = part_im.astype(BF16)
            lhs_ref[top, band:] = (-part_im).astype(BF16)

    scale = 1.0 / math.sqrt(band)
    fine_c, fine_s = trig_ref[24:32, :], trig_ref[56:64, :]
    base_c, base_s = [], []
    for b in range(8):
        c, s = trig_ref[16 + b : 17 + b, :], trig_ref[48 + b : 49 + b, :]
        base_c.append((c * fine_c - s * fine_s) * scale)
        base_s.append((s * fine_c + c * fine_s) * scale)
    base_c = jnp.concatenate(base_c, axis=0)
    base_s = jnp.concatenate(base_s, axis=0)
    for a in range(16):
        c, s = trig_ref[a : a + 1, :], trig_ref[32 + a : 33 + a, :]
        cos_ref[64 * a : 64 * a + 64, :] = (c * base_c - s * base_s).astype(BF16)
        sin_ref[64 * a : 64 * a + 64, :] = (s * base_c + c * base_s).astype(BF16)
    product = jnp.dot(lhs_ref[:, :band], cos_ref[...], preferred_element_type=F32)
    product += jnp.dot(lhs_ref[:, band:], sin_ref[...], preferred_element_type=F32)
    scatter_blocks(product, out_ref)


def field_kernel(w_ref, in_ref, cos_ref, sin_ref, field_ref, power_ref, lhs_ref):
    band = in_ref.shape[0]
    half = in_ref.shape[1] // 2
    points = w_ref.shape[0]
    rows = half // points

    @pl.when(pl.program_id(0) == 0)
    def _():
        for k in range(0, band, CHUNK):
            turned = in_ref[k : k + CHUNK, :].T
            lhs_ref[:, k : k + CHUNK] = turned
            lhs_ref[:half, band + k : band + k + CHUNK] = -turned[half:]
            lhs_ref[half:, band + k : band + k + CHUNK] = turned[:half]

    product = jnp.dot(lhs_ref[:, :band], cos_ref[...], preferred_element_type=F32)
    product += jnp.dot(lhs_ref[:, band:], sin_ref[...], preferred_element_type=F32)
    field_ref[...] = product
    total = jnp.zeros((rows, CHUNK), F32)
    for p in range(points):
        re = product[p * rows : (p + 1) * rows]
        im = product[half + p * rows : half + (p + 1) * rows]
        total += w_ref[p] * (re * re + im * im)
    for block in range(4):
        for side in range(2):
            power_ref[block, 0, 8 * side : 8 * side + 8, :] = total[
                8 * block : 8 * block + 8, side * LANES : (side + 1) * LANES
            ]


def adjoint_kernel(total_points, w_ref, power_ref, target_ref, field_ref, cos_ref, sin_ref, out_ref, lhs_ref):
    rows, band = target_ref.shape
    points = w_ref.shape[0]
    half = rows * points

    @pl.when(pl.program_id(0) == 0)
    def _():
        for n in range(4):
            cols = slice(n * CHUNK, (n + 1) * CHUNK)
            power = jnp.concatenate(
                [
                    jnp.concatenate([power_ref[block, n, :8, :], power_ref[block, n, 8:, :]], axis=1)
                    for block in range(4)
                ],
                axis=0,
            )
            mismatch = power * (1.0 / total_points) - target_ref[:, cols]
            shifted = slice(band + n * CHUNK, band + (n + 1) * CHUNK)
            for p in range(points):
                top = slice(p * rows, (p + 1) * rows)
                low = slice(half + p * rows, half + (p + 1) * rows)
                factor = (2.0 * w_ref[p]) * mismatch
                grad_re = factor * field_ref[top, cols]
                grad_im = factor * field_ref[low, cols]
                lhs_ref[top, cols] = grad_re.astype(BF16)
                lhs_ref[top, shifted] = grad_im.astype(BF16)
                lhs_ref[low, cols] = grad_im.astype(BF16)
                lhs_ref[low, shifted] = (-grad_re).astype(BF16)

    product = jnp.dot(lhs_ref[:, :band], cos_ref[...], preferred_element_type=F32)
    product += jnp.dot(lhs_ref[:, band:], sin_ref[...], preferred_element_type=F32)
    scatter_blocks(product, out_ref)


def gradient_kernel(row_ref, cr_ref, cc_ref, in_ref, cos_ref, sin_ref, out_ref, lhs_ref):
    step = pl.program_id(0)
    band = in_ref.shape[0]
    half = in_ref.shape[1] // 2
    points = cr_ref.shape[0]
    rows = half // points

    @pl.when(step == 0)
    def _():
        for k in range(0, band, CHUNK):
            turned = in_ref[k : k + CHUNK, :].T
            lhs_ref[:, k : k + CHUNK] = turned
            lhs_ref[:half, band + k : band + k + CHUNK] = turned[half:]
            lhs_ref[half:, band + k : band + k + CHUNK] = -turned[:half]

    product = jnp.dot(lhs_ref[:, :band], cos_ref[...], preferred_element_type=F32)
    product += jnp.dot(lhs_ref[:, band:], sin_ref[...], preferred_element_type=F32)
    total_re = jnp.zeros((rows, CHUNK), F32)
    total_im = jnp.zeros((rows, CHUNK), F32)
    for p in range(points):
        keep = inside(row_ref[0] * rows, step * CHUNK, (rows, CHUNK), cr_ref[p], cc_ref[p])
        total_re += jnp.where(keep, product[p * rows : (p + 1) * rows], 0.0)
        total_im += jnp.where(keep, product[half + p * rows : half + (p + 1) * rows], 0.0)
    for side in range(2):
        lanes = slice(side * LANES, (side + 1) * LANES)
        out_ref[0, side] = total_re[:, lanes].astype(BF16)
        out_ref[1, side] = total_im[:, lanes].astype(BF16)


def sum_kernel(in_ref, out_ref):
    total = in_ref[0].astype(F32)
    for i in range(1, in_ref.shape[0]):
        total += in_ref[i].astype(F32)
    total = total.astype(out_ref.dtype)
    for i in range(out_ref.shape[0]):
        out_ref[i] = total


def unpack_kernel(in_ref, re_ref, im_ref):
    for tile in range(8):
        lanes = slice(tile * LANES, (tile + 1) * LANES)
        re_ref[:, lanes] = in_ref[tile].astype(F32)
        im_ref[:, lanes] = in_ref[8 + tile].astype(F32)


def table_spec(band):
    return pl.BlockSpec((band, CHUNK), lambda n: (0, n))


def exchange(value, axis):
    return lax.all_to_all(value, axis, split_axis=0, concat_axis=0, tiled=True)


def sum_everywhere(value):
    received = exchange(value, "src")
    summed = pl.pallas_call(
        sum_kernel, out_shape=jax.ShapeDtypeStruct(value.shape, value.dtype), name="sum_parts"
    )(received)
    return exchange(summed, "src")


def local(spec_re, spec_im, target, weights, cent_row, cent_col):
    rows, band = spec_re.shape
    points = weights.shape[0]
    total_points = points * lax.axis_size("src")
    devices = lax.axis_size("row")
    wide = 2 * points * rows
    steps = band // CHUNK
    row = lax.axis_index("row").astype(jnp.int32).reshape(1)
    table = jax.ShapeDtypeStruct((band, band), BF16)
    parts = jax.ShapeDtypeStruct((devices, rows, wide), BF16)
    parts_spec = pl.BlockSpec((devices // steps, rows, wide), lambda n: (n, 0, 0))
    lhs = pltpu.VMEM((wide, 2 * band), BF16)

    cosine, sine, column_parts = pl.pallas_call(
        spectrum_kernel,
        grid=(steps,),
        in_specs=[SCALARS, SCALARS, SCALARS, pl.BlockSpec((64, CHUNK), lambda n: (0, n)), WHOLE, WHOLE],
        out_specs=[table_spec(band), table_spec(band), parts_spec],
        out_shape=[table, table, parts],
        scratch_shapes=[lhs],
        name="spectrum",
    )(row, cent_row, cent_col, trig_rows(band), spec_re, spec_im)
    columns = exchange(column_parts, "row").reshape(band, wide)
    field, power = pl.pallas_call(
        field_kernel,
        grid=(steps,),
        in_specs=[SCALARS, WHOLE, table_spec(band), table_spec(band)],
        out_specs=[
            pl.BlockSpec((wide, CHUNK), lambda n: (0, n)),
            pl.BlockSpec((4, 1, 16, LANES), lambda n: (0, n, 0, 0)),
        ],
        out_shape=[
            jax.ShapeDtypeStruct((wide, band), F32),
            jax.ShapeDtypeStruct((4, 4, 16, LANES), F32),
        ],
        scratch_shapes=[lhs],
        name="field",
    )(weights, columns, cosine, sine)
    power = sum_everywhere(power.reshape(16, 16, LANES)).reshape(4, 4, 16, LANES)
    adjoint_parts = pl.pallas_call(
        functools.partial(adjoint_kernel, total_points),
        grid=(steps,),
        in_specs=[SCALARS, WHOLE, WHOLE, WHOLE, table_spec(band), table_spec(band)],
        out_specs=parts_spec,
        out_shape=parts,
        scratch_shapes=[lhs],
        name="adjoint",
    )(weights, power, target, field, cosine, sine)
    adjoint = exchange(adjoint_parts, "row").reshape(band, wide)
    gradient = pl.pallas_call(
        gradient_kernel,
        grid=(steps,),
        in_specs=[SCALARS, SCALARS, SCALARS, WHOLE, table_spec(band), table_spec(band)],
        out_specs=pl.BlockSpec((2, 2, rows, LANES), lambda n: (0, n, 0, 0)),
        out_shape=jax.ShapeDtypeStruct((2, 8, rows, LANES), BF16),
        scratch_shapes=[lhs],
        name="gradient",
    )(row, cent_row, cent_col, adjoint, cosine, sine)
    gradient = sum_everywhere(gradient.reshape(16, rows, LANES))
    out = jax.ShapeDtypeStruct((rows, band), F32)
    return tuple(pl.pallas_call(unpack_kernel, out_shape=[out, out], name="unpack")(gradient))


def solution(mesh):
    return jax.shard_map(
        local,
        mesh=mesh,
        in_specs=(P("row", None), P("row", None), P("row", None), P("src"), P("src"), P("src")),
        out_specs=(P("row", None), P("row", None)),
        check_vma=False,
    )
```

```python
import math

import jax
import jax.numpy as jnp
from jax import lax
from jax.experimental import pallas as pl
from jax.experimental.pallas import tpu as pltpu
from jax.sharding import PartitionSpec as P

RAD = 128
F32 = jnp.float32
BF16 = jnp.bfloat16
CHUNK = 256
LANES = 128
STEPS = 4

WHOLE = pl.BlockSpec(memory_space=pltpu.VMEM)
SCALARS = pl.BlockSpec(memory_space=pltpu.SMEM)


def trig_rows(band):
    index = jnp.arange(64, dtype=jnp.int32)
    rows = jnp.where(index < 32, index, 32 * (index - 32))
    phase = rows[:, None] * jnp.arange(band, dtype=jnp.int32)[None, :]
    both = jnp.concatenate([phase, phase + (band - band // 4)], axis=0) % band
    return jnp.cos(both.astype(F32) * (2.0 * math.pi / band))


def dot_nt(left, right):
    return lax.dot_general(left, right, (((1,), (1,)), ((), ())), preferred_element_type=F32)


def dot_nn(left, right):
    return jnp.dot(left, right, preferred_element_type=F32)


def spectrum_kernel(row_ref, info_ref, trig_ref, re_ref, im_ref, cos_ref, sin_ref, out_ref, lhs_ref, flat_ref):
    step = pl.program_id(0)
    rows, band = re_ref.shape

    @pl.when(step == 0)
    def _():
        spec_re = re_ref[...].astype(F32)
        spec_im = im_ref[...].astype(F32)
        info = info_ref[0]
        centre_row, centre_col = info[:, 1:2], info[:, 2:3]
        col_gap = lax.broadcasted_iota(jnp.int32, (8, band), 1).astype(F32) - centre_col
        col_gap = col_gap * col_gap
        first = (row_ref[0] * rows).astype(F32)
        for k in range(rows):
            row_gap = first + float(k) - centre_row
            keep = row_gap * row_gap + col_gap <= float(RAD * RAD)
            part_re = jnp.where(keep, spec_re[k : k + 1, :], 0.0)
            part_im = jnp.where(keep, spec_im[k : k + 1, :], 0.0)
            place = slice(16 * k, 16 * k + 16)
            lhs_ref[place, :band] = jnp.concatenate([part_re, part_im], axis=0).astype(BF16)
            lhs_ref[place, band:] = jnp.concatenate([-part_im, part_re], axis=0).astype(BF16)

    scale = 1.0 / math.sqrt(band)
    base_c, base_s = trig_ref[0:32, :] * scale, trig_ref[64:96, :] * scale
    turn_c = trig_ref[pl.ds(pl.multiple_of(32 + 8 * step, 8), 8), :]
    turn_s = trig_ref[pl.ds(pl.multiple_of(96 + 8 * step, 8), 8), :]
    for r in range(8):
        c, s = turn_c[r : r + 1, :], turn_s[r : r + 1, :]
        cos_ref[32 * r : 32 * r + 32, :] = (c * base_c - s * base_s).astype(BF16)
        sin_ref[32 * r : 32 * r + 32, :] = (s * base_c + c * base_s).astype(BF16)
    product = dot_nt(cos_ref[...], lhs_ref[:, :band]) + dot_nt(sin_ref[...], lhs_ref[:, band:])
    for t in range(4):
        flat_ref[pl.ds(t, CHUNK, stride=4), :] = product[:, t * LANES : (t + 1) * LANES]
    low_row = lax.broadcasted_iota(jnp.int32, (8, LANES), 0) < 4
    low_lane = lax.broadcasted_iota(jnp.int32, (8, LANES), 1) < 64
    stay = low_row == low_lane
    for r in range(8):
        for s in range(16):
            first_row = 8 * (16 * r + s)
            tile = flat_ref[first_row : first_row + 8, :]
            moved = pltpu.roll(pltpu.roll(tile, 4, 0), 64, 1)
            out_ref[s, r] = jnp.where(stay, tile, moved).astype(BF16)


def tables_kernel(trig_ref, cos_k_ref, sin_k_ref, cos_y_ref, sin_y_ref):
    scale = 1.0 / math.sqrt(4 * trig_ref.shape[1])
    base_c, base_s = trig_ref[0:32, :] * scale, trig_ref[64:96, :] * scale
    turn_c, turn_s = trig_ref[32:64, :], trig_ref[96:128, :]
    for j in range(4):
        order = [j + 8 * (i % 4) + 4 * (i // 4) for i in range(8)]
        near_c = jnp.concatenate([base_c[f : f + 1, :] for f in order], axis=0)
        near_s = jnp.concatenate([base_s[f : f + 1, :] for f in order], axis=0)
        for r in range(0, 32, 2):
            cs, ss = [], []
            for turn in (r, r + 1):
                c, s = turn_c[turn : turn + 1, :], turn_s[turn : turn + 1, :]
                cs.append(c * near_c - s * near_s)
                ss.append(s * near_c + c * near_s)
            place = slice(256 * j + 8 * r, 256 * j + 8 * r + 16)
            cos_k_ref[place, :] = jnp.concatenate(cs, axis=0).astype(BF16)
            sin_k_ref[place, :] = jnp.concatenate(ss, axis=0).astype(BF16)
    for f in range(32):
        c, s = base_c[f : f + 1, :], base_s[f : f + 1, :]
        first = 512 * (f % 2) + 32 * (f // 2)
        cos_y_ref[first : first + 32, :] = (c * turn_c - s * turn_s).astype(BF16)
        sin_y_ref[first : first + 32, :] = (s * turn_c + c * turn_s).astype(BF16)


def image_kernel(
    src_ref, info_ref, in_ref, target_ref, cos_k_ref, sin_k_ref, cos_ref, sin_ref, out_ref, lhs_ref, grad_ref, flat_ref
):
    step = pl.program_id(0)

    @pl.when(step == 0)
    def _():
        for s in range(16):
            turned = in_ref[256 * s : 256 * s + 256, :].T
            for y in range(2):
                for j in range(4):
                    lhs_ref[32 * s + 16 * y : 32 * s + 16 * y + 16, 256 * j : 256 * j + 256] = turned[
                        64 * y + 16 * j : 64 * y + 16 * j + 16
                    ]

    @pl.when(step < STEPS)
    def _():
        by_cos = dot_nn(lhs_ref[...], cos_k_ref[...])
        by_sin = dot_nn(lhs_ref[...], sin_k_ref[...])

        def field(s, y):
            at = 32 * s + 16 * y
            re = by_cos[at : at + 8] - by_sin[at + 8 : at + 16]
            im = by_sin[at : at + 8] + by_cos[at + 8 : at + 16]
            return re, im

        for y in range(2):
            power = jnp.zeros((8, CHUNK), F32)
            for s in range(16):
                re, im = field(s, y)
                power += info_ref[s, :, 0:1] * (re * re + im * im)
            intensity = jnp.sum(power, axis=0, keepdims=True) * (1.0 / 128.0)
            mismatch = intensity - target_ref[pl.ds(2 * src_ref[0] + y, 1), :]
            for s in range(0, 16, 2):
                grads_re, grads_im = [], []
                for one in (s, s + 1):
                    re, im = field(one, y)
                    factor = (2.0 * info_ref[one, :, 0:1]) * mismatch
                    grads_re.append(factor * re)
                    grads_im.append(factor * im)
                at = 256 * y + 8 * s
                grad_ref[step, at : at + 16, :] = jnp.concatenate(grads_re, axis=0).astype(BF16)
                grad_ref[step, at + 128 : at + 144, :] = jnp.concatenate(grads_im, axis=0).astype(BF16)

    @pl.when(step >= STEPS)
    def _():
        by_cos = jnp.zeros((CHUNK, 512), F32)
        by_sin = jnp.zeros((CHUNK, 512), F32)
        for n in range(STEPS):
            cols = slice(n * CHUNK, (n + 1) * CHUNK)
            by_cos += dot_nt(cos_ref[:, cols], grad_ref[n])
            by_sin += dot_nt(sin_ref[:, cols], grad_ref[n])
        for y in range(2):
            re, im = slice(256 * y, 256 * y + 128), slice(256 * y + 128, 256 * y + 256)
            flat_ref[pl.ds(2 * y, CHUNK, stride=4), :] = by_cos[:, re] + by_sin[:, im]
            flat_ref[pl.ds(2 * y + 1, CHUNK, stride=4), :] = by_cos[:, im] - by_sin[:, re]
        for r in range(8):
            for s in range(16):
                first_row = 8 * (16 * r + s)
                out_ref[s, r] = flat_ref[first_row : first_row + 8, :].astype(BF16)


def gradient_kernel(place_ref, info_ref, in_ref, cos_ref, sin_ref, out_ref, lhs_ref, flat_ref, sums_ref):
    step = pl.program_id(0)

    @pl.when(step == 0)
    def _():
        for first in range(0, 4096, 512):
            flat_ref[first : first + 512, :] = in_ref[first : first + 512, :].astype(F32)
        for k in range(2):
            for y in range(2):
                for c in range(2):
                    part = flat_ref[pl.ds(4 * k + 2 * y + c, 512, stride=8), :]
                    lhs_ref[128 * (2 * c + k) : 128 * (2 * c + k) + 128, 512 * y : 512 * y + 512] = part.T.astype(BF16)

    by_cos = dot_nn(lhs_ref[...], cos_ref[...])
    by_sin = dot_nn(lhs_ref[...], sin_ref[...])
    centre_row, centre_col = info_ref[:, 1:2], info_ref[:, 2:3]
    first_col = (step * CHUNK).astype(F32)
    col_gap = lax.broadcasted_iota(jnp.int32, (LANES, CHUNK), 1).astype(F32) + (first_col - centre_col)
    col_gap = col_gap * col_gap
    for k in range(2):
        row_gap = (place_ref[0] + k).astype(F32) - centre_row
        keep = row_gap * row_gap + col_gap <= float(RAD * RAD)
        re, im = slice(128 * k, 128 * k + 128), slice(256 + 128 * k, 256 + 128 * k + 128)
        terms = (by_cos[re] + by_sin[im], by_cos[im] - by_sin[re])
        for c in range(2):
            total = jnp.sum(jnp.where(keep, terms[c], 0.0), axis=0, keepdims=True)
            for side in range(2):
                sums_ref[pl.ds(16 * k + 8 * c + 2 * step + side, 1), :] = total[:, side * LANES : (side + 1) * LANES]

    @pl.when(step == STEPS - 1)
    def _():
        for i in range(16):
            out_ref[i] = sums_ref[...].astype(BF16)


def unpack_kernel(in_ref, re_ref, im_ref, flat_ref):
    flat_ref[...] = in_ref[...].astype(F32)
    for c, ref in enumerate((re_ref, im_ref)):
        for tile in range(8):
            ref[:, tile * LANES : (tile + 1) * LANES] = flat_ref[pl.ds(8 * c + tile, 32, stride=16), :]


def exchange(value, axis):
    return lax.all_to_all(value, axis, split_axis=0, concat_axis=0, tiled=True)


def local(spec_re, spec_im, target, weights, cent_row, cent_col):
    rows, band = spec_re.shape
    everyone = ("src", "row")
    row = lax.axis_index("row").astype(jnp.int32).reshape(1)
    src = lax.axis_index("src").astype(jnp.int32).reshape(1)
    lane = lax.broadcasted_iota(jnp.int32, (16, 8, LANES), 2)
    info = jnp.where(lane == 1, cent_row.astype(F32)[None, :, None], cent_col.astype(F32)[None, :, None])
    info = jnp.where(lane == 0, weights[None, :, None], info)
    trig = trig_rows(band)
    table = jax.ShapeDtypeStruct((band, band), BF16)
    parts = jax.ShapeDtypeStruct((16, 32, 8, LANES), BF16)
    row_block = pl.BlockSpec((CHUNK, band), lambda n: (n, 0))
    col_block = pl.BlockSpec((band, CHUNK), lambda n: (0, n))

    all_info = exchange(info, "src")
    cosine, sine, column_parts = pl.pallas_call(
        spectrum_kernel,
        grid=(STEPS,),
        in_specs=[SCALARS, WHOLE, WHOLE, WHOLE, WHOLE],
        out_specs=[row_block, row_block, pl.BlockSpec((16, 8, 8, LANES), lambda n: (0, n, 0, 0))],
        out_shape=[table, table, parts],
        scratch_shapes=[pltpu.VMEM((512, 2 * band), BF16), pltpu.VMEM((4 * CHUNK, LANES), F32)],
        name="spectrum",
    )(row, info, trig, spec_re, spec_im)
    cos_k, sin_k, cos_y, sin_y = pl.pallas_call(
        tables_kernel,
        grid=(STEPS,),
        in_specs=[pl.BlockSpec((128, CHUNK), lambda n: (0, n))],
        out_specs=[col_block] * 4,
        out_shape=[table] * 4,
        cost_estimate=pl.CostEstimate(flops=12 * band * band, bytes_accessed=8 * band * band, transcendentals=0),
        name="tables",
    )(trig)
    columns = exchange(column_parts.reshape(512, 8, LANES), everyone).reshape(4096, LANES)
    adjoint_parts = pl.pallas_call(
        image_kernel,
        grid=(2 * STEPS,),
        in_specs=[
            SCALARS,
            WHOLE,
            WHOLE,
            pl.BlockSpec((rows, CHUNK), lambda n: (0, jnp.minimum(n, STEPS - 1))),
            pl.BlockSpec((band, CHUNK), lambda n: (0, jnp.minimum(n, STEPS - 1))),
            pl.BlockSpec((band, CHUNK), lambda n: (0, jnp.minimum(n, STEPS - 1))),
            pl.BlockSpec((CHUNK, band), lambda n: (jnp.maximum(n - STEPS, 0), 0)),
            pl.BlockSpec((CHUNK, band), lambda n: (jnp.maximum(n - STEPS, 0), 0)),
        ],
        out_specs=pl.BlockSpec((16, 8, 8, LANES), lambda n: (0, jnp.maximum(n - STEPS, 0), 0, 0)),
        out_shape=parts,
        scratch_shapes=[
            pltpu.VMEM((512, band), BF16),
            pltpu.VMEM((STEPS, 512, CHUNK), BF16),
            pltpu.VMEM((4 * CHUNK, LANES), F32),
        ],
        name="image",
    )(src, all_info, columns, target, cos_k, sin_k, cosine, sine)
    adjoint = exchange(adjoint_parts.reshape(512, 8, LANES), everyone).reshape(4096, LANES)
    gradient = pl.pallas_call(
        gradient_kernel,
        grid=(STEPS,),
        in_specs=[SCALARS, WHOLE, WHOLE, col_block, col_block],
        out_specs=WHOLE,
        out_shape=jax.ShapeDtypeStruct((16, 32, LANES), BF16),
        scratch_shapes=[
            pltpu.VMEM((512, band), BF16),
            pltpu.VMEM((4096, LANES), F32),
            pltpu.VMEM((32, LANES), F32),
        ],
        name="gradient",
    )(row * rows + 2 * src, all_info.reshape(LANES, LANES), adjoint, cos_y, sin_y)
    gradient = exchange(gradient, "src").reshape(512, LANES)
    out = jax.ShapeDtypeStruct((rows, band), F32)
    return tuple(
        pl.pallas_call(
            unpack_kernel, out_shape=[out, out], scratch_shapes=[pltpu.VMEM((512, LANES), F32)], name="unpack"
        )(gradient)
    )


def solution(mesh):
    return jax.shard_map(
        local,
        mesh=mesh,
        in_specs=(P("row", None), P("row", None), P("row", None), P("src"), P("src"), P("src")),
        out_specs=(P("row", None), P("row", None)),
        check_vma=False,
    )
```

```python
import math

import jax
import jax.numpy as jnp
from jax import lax
from jax.experimental import pallas as pl
from jax.experimental.pallas import tpu as pltpu
from jax.sharding import PartitionSpec as P


RAD = 128
F32 = jnp.float32
BF16 = jnp.bfloat16
CHUNK = 256
WIDE = 512
LANES = 128
STEPS = 4

WHOLE = pl.BlockSpec(memory_space=pltpu.VMEM)
SCALARS = pl.BlockSpec(memory_space=pltpu.SMEM)


def trig_rows(band):
    index = jnp.arange(24, dtype=jnp.int32)
    rows = jnp.where(index < 8, index, 128 * (index - 8))
    rows = jnp.where(index < 16, rows, jnp.where(index < 20, 8 * (index - 16), 32 * (index - 20)))
    phase = rows[:, None] * jnp.arange(band, dtype=jnp.int32)[None, :]
    both = jnp.concatenate([phase, phase + (band - band // 4)], axis=0) % band
    return jnp.cos(both.astype(F32) * (2.0 * math.pi / band))


def rotate(one, other):
    return one[0] * other[0] - one[1] * other[1], one[1] * other[0] + one[0] * other[1]


def pick(trig, first, count=1):
    return trig[first : first + count, :], trig[24 + first : 24 + first + count, :]


def base_rows(trig, scale):
    fine = tuple(part * scale for part in pick(trig, 0, 8))
    blocks = [rotate(pick(trig, 16 + b), fine) for b in range(4)]
    return tuple(jnp.concatenate([block[i] for block in blocks], axis=0) for i in range(2))


def info_tile(w_ref, cr_ref, cc_ref):
    shape = (8, LANES)
    sublane = lax.broadcasted_iota(jnp.int32, shape, 0)
    lane = lax.broadcasted_iota(jnp.int32, shape, 1)
    tile = jnp.zeros(shape, F32)
    for p in range(8):
        centre = jnp.where(lane == 1, cr_ref[p].astype(F32), cc_ref[p].astype(F32))
        tile = jnp.where(sublane == p, jnp.where(lane == 0, w_ref[p], centre), tile)
    return tile


def dot_nt(left, right):
    return lax.dot_general(left, right, (((1,), (1,)), ((), ())), preferred_element_type=F32)


def dot_nn(left, right):
    return jnp.dot(left, right, preferred_element_type=F32)


def spectrum_kernel(row_ref, w_ref, cr_ref, cc_ref, trig_ref, re_ref, im_ref, out_ref, lhs_ref, cos_ref, sin_ref, flat_ref):
    step = pl.program_id(0)
    rows, band = re_ref.shape

    @pl.when(step == 0)
    def _():
        spec_re = re_ref[...].astype(F32)
        spec_im = im_ref[...].astype(F32)
        info = info_tile(w_ref, cr_ref, cc_ref)
        centre_row, centre_col = info[:, 1:2], info[:, 2:3]
        col_gap = lax.broadcasted_iota(jnp.int32, (8, band), 1).astype(F32) - centre_col
        col_gap = col_gap * col_gap
        first = (row_ref[0] * rows).astype(F32)
        for k in range(rows):
            row_gap = first + float(k) - centre_row
            keep = row_gap * row_gap + col_gap <= float(RAD * RAD)
            part_re = jnp.where(keep, spec_re[k : k + 1, :], 0.0)
            part_im = jnp.where(keep, spec_im[k : k + 1, :], 0.0)
            place = slice(16 * k, 16 * k + 16)
            lhs_ref[place, :band] = jnp.concatenate([part_re, part_im], axis=0).astype(BF16)
            lhs_ref[place, band:] = jnp.concatenate([-part_im, part_re], axis=0).astype(BF16)

    base = base_rows(trig_ref, 1.0 / math.sqrt(band))
    for a in range(4):
        coarse = tuple(trig_ref[pl.ds(first + 4 * step + a, 1), :] for first in (8, 32))
        for d in range(4):
            cos, sin = rotate(rotate(coarse, pick(trig_ref, 20 + d)), base)
            place = slice(128 * a + 32 * d, 128 * a + 32 * d + 32)
            cos_ref[place, :] = cos.astype(BF16)
            sin_ref[place, :] = sin.astype(BF16)
    product = dot_nt(cos_ref[...], lhs_ref[:, :band]) + dot_nt(sin_ref[...], lhs_ref[:, band:])
    for t in range(4):
        flat_ref[pl.ds(t, WIDE, stride=4), :] = product[:, t * LANES : (t + 1) * LANES]
    low_row = lax.broadcasted_iota(jnp.int32, (8, LANES), 0) < 4
    low_lane = lax.broadcasted_iota(jnp.int32, (8, LANES), 1) < 64
    stay = low_row == low_lane
    for r in range(16):
        for s in range(16):
            first_row = 8 * (16 * r + s)
            tile = flat_ref[first_row : first_row + 8, :]
            moved = pltpu.roll(pltpu.roll(tile, 4, 0), 64, 1)
            out_ref[s, r] = jnp.where(stay, tile, moved).astype(BF16)


def tables_kernel(
    w_ref, cr_ref, cc_ref, trig_ref, _, info_ref, cos_ref, sin_ref, cos_k_ref, sin_k_ref, cos_y_ref, sin_y_ref
):
    @pl.when(pl.program_id(0) == 0)
    def _():
        info_ref[0] = info_tile(w_ref, cr_ref, cc_ref)

    base_c, base_s = base_rows(trig_ref, 1.0 / math.sqrt(4 * trig_ref.shape[1]))
    turns = [rotate(pick(trig_ref, 8 + a), pick(trig_ref, 20 + d)) for a in range(8) for d in range(4)]
    turn_c, turn_s = (jnp.concatenate([turn[i] for turn in turns], axis=0) for i in range(2))
    for r in range(32):
        cos, sin = rotate(turns[r], (base_c, base_s))
        cos_ref[32 * r : 32 * r + 32, :] = cos.astype(BF16)
        sin_ref[32 * r : 32 * r + 32, :] = sin.astype(BF16)
    for j in range(4):
        order = [j + 8 * (i % 4) + 4 * (i // 4) for i in range(8)]
        near_c = jnp.concatenate([base_c[f : f + 1, :] for f in order], axis=0)
        near_s = jnp.concatenate([base_s[f : f + 1, :] for f in order], axis=0)
        for r in range(0, 32, 2):
            cs, ss = [], []
            for turn in (r, r + 1):
                c, s = turn_c[turn : turn + 1, :], turn_s[turn : turn + 1, :]
                cs.append(c * near_c - s * near_s)
                ss.append(s * near_c + c * near_s)
            place = slice(256 * j + 8 * r, 256 * j + 8 * r + 16)
            cos_k_ref[place, :] = jnp.concatenate(cs, axis=0).astype(BF16)
            sin_k_ref[place, :] = jnp.concatenate(ss, axis=0).astype(BF16)
    for f in range(32):
        c, s = base_c[f : f + 1, :], base_s[f : f + 1, :]
        first = 512 * (f % 2) + 32 * (f // 2)
        cos_y_ref[first : first + 32, :] = (c * turn_c - s * turn_s).astype(BF16)
        sin_y_ref[first : first + 32, :] = (s * turn_c + c * turn_s).astype(BF16)


def image_kernel(
    src_ref, info_ref, in_ref, target_ref, cos_k_ref, sin_k_ref, cos_ref, sin_ref, out_ref, lhs_ref, grad_ref, flat_ref
):
    step = pl.program_id(0)

    def weight(s):
        return info_ref[jnp.bitwise_xor(src_ref[0], s)][:, 0:1]

    @pl.when(step == 0)
    def _():
        for s in range(16):
            turned = in_ref[256 * s : 256 * s + 256, :].T
            for y in range(2):
                for j in range(4):
                    lhs_ref[32 * s + 16 * y : 32 * s + 16 * y + 16, 256 * j : 256 * j + 256] = turned[
                        64 * y + 16 * j : 64 * y + 16 * j + 16
                    ]

    @pl.when(step < STEPS)
    def _():
        by_cos = dot_nn(lhs_ref[...], cos_k_ref[...])
        by_sin = dot_nn(lhs_ref[...], sin_k_ref[...])

        def field(s, y):
            at = 32 * s + 16 * y
            re = by_cos[at : at + 8] - by_sin[at + 8 : at + 16]
            im = by_sin[at : at + 8] + by_cos[at + 8 : at + 16]
            return re, im

        for y in range(2):
            power = jnp.zeros((8, CHUNK), F32)
            for s in range(16):
                re, im = field(s, y)
                power += weight(s) * (re * re + im * im)
            intensity = jnp.sum(power, axis=0, keepdims=True) * (1.0 / 128.0)
            mismatch = intensity - target_ref[pl.ds(2 * src_ref[0] + y, 1), :]
            for s in range(0, 16, 2):
                grads_re, grads_im = [], []
                for one in (s, s + 1):
                    re, im = field(one, y)
                    factor = (2.0 * weight(one)) * mismatch
                    grads_re.append(factor * re)
                    grads_im.append(factor * im)
                at = 256 * y + 8 * s
                grad_ref[step, at : at + 16, :] = jnp.concatenate(grads_re, axis=0).astype(BF16)
                grad_ref[step, at + 128 : at + 144, :] = jnp.concatenate(grads_im, axis=0).astype(BF16)

    @pl.when(step >= STEPS)
    def _():
        by_cos = jnp.zeros((WIDE, 512), F32)
        by_sin = jnp.zeros((WIDE, 512), F32)
        for n in range(STEPS):
            cols = slice(n * CHUNK, (n + 1) * CHUNK)
            by_cos += dot_nt(cos_ref[:, cols], grad_ref[n])
            by_sin += dot_nt(sin_ref[:, cols], grad_ref[n])
        for y in range(2):
            re, im = slice(256 * y, 256 * y + 128), slice(256 * y + 128, 256 * y + 256)
            flat_ref[pl.ds(2 * y, WIDE, stride=4), :] = by_cos[:, re] + by_sin[:, im]
            flat_ref[pl.ds(2 * y + 1, WIDE, stride=4), :] = by_cos[:, im] - by_sin[:, re]
        for r in range(16):
            for s in range(16):
                first_row = 8 * (16 * r + s)
                out_ref[s, r] = flat_ref[first_row : first_row + 8, :].astype(BF16)


def gradient_kernel(place_ref, src_ref, info_ref, in_ref, cos_ref, sin_ref, out_ref, lhs_ref, flat_ref, sums_ref):
    step = pl.program_id(0)

    @pl.when(step == 0)
    def _():
        for first in range(0, 4096, 512):
            flat_ref[first : first + 512, :] = in_ref[first : first + 512, :].astype(F32)
        for k in range(2):
            for y in range(2):
                for c in range(2):
                    part = flat_ref[pl.ds(4 * k + 2 * y + c, 512, stride=8), :]
                    lhs_ref[128 * (2 * c + k) : 128 * (2 * c + k) + 128, 512 * y : 512 * y + 512] = part.T.astype(BF16)

    by_cos = dot_nn(lhs_ref[...], cos_ref[...])
    by_sin = dot_nn(lhs_ref[...], sin_ref[...])
    info = jnp.concatenate([info_ref[jnp.bitwise_xor(src_ref[0], s)] for s in range(16)], axis=0)
    centre_row, centre_col = info[:, 1:2], info[:, 2:3]
    first_col = (step * CHUNK).astype(F32)
    col_gap = lax.broadcasted_iota(jnp.int32, (LANES, CHUNK), 1).astype(F32) + (first_col - centre_col)
    col_gap = col_gap * col_gap
    for k in range(2):
        row_gap = (place_ref[0] + k).astype(F32) - centre_row
        keep = row_gap * row_gap + col_gap <= float(RAD * RAD)
        re, im = slice(128 * k, 128 * k + 128), slice(256 + 128 * k, 256 + 128 * k + 128)
        terms = (by_cos[re] + by_sin[im], by_cos[im] - by_sin[re])
        for c in range(2):
            total = jnp.sum(jnp.where(keep, terms[c], 0.0), axis=0, keepdims=True)
            for side in range(2):
                sums_ref[pl.ds(16 * k + 8 * c + 2 * step + side, 1), :] = total[:, side * LANES : (side + 1) * LANES]

    @pl.when(step == STEPS - 1)
    def _():
        for i in range(16):
            out_ref[i] = sums_ref[...].astype(BF16)


def unpack_kernel(in_ref, re_ref, im_ref, flat_ref):
    flat_ref[...] = in_ref[...].astype(F32)
    for c, ref in enumerate((re_ref, im_ref)):
        for tile in range(8):
            ref[:, tile * LANES : (tile + 1) * LANES] = flat_ref[pl.ds(8 * c + tile, 32, stride=16), :]


def exchange(value, axis):
    return lax.all_to_all(value, axis, split_axis=0, concat_axis=0, tiled=True)


def gather_info(info):
    for bit in (1, 2, 4, 8):
        info = jnp.concatenate([info, lax.ppermute(info, "src", [(i, i ^ bit) for i in range(16)])], axis=0)
    return info


def compute(spec_re, spec_im, target, weights, cent_row, cent_col):
    rows, band = spec_re.shape
    everyone = ("src", "row")
    row = lax.axis_index("row").astype(jnp.int32).reshape(1)
    src = lax.axis_index("src").astype(jnp.int32).reshape(1)
    trig = trig_rows(band)
    table = jax.ShapeDtypeStruct((band, band), BF16)
    parts = jax.ShapeDtypeStruct((16, 32, 8, LANES), BF16)
    col_block = pl.BlockSpec((band, CHUNK), lambda n: (0, n))
    scalars = (weights, cent_row, cent_col)

    column_parts = pl.pallas_call(
        spectrum_kernel,
        grid=(2,),
        in_specs=[SCALARS, SCALARS, SCALARS, SCALARS, WHOLE, WHOLE, WHOLE],
        out_specs=pl.BlockSpec((16, 16, 8, LANES), lambda n: (0, n, 0, 0)),
        out_shape=parts,
        scratch_shapes=[
            pltpu.VMEM((512, 2 * band), BF16),
            pltpu.VMEM((WIDE, band), BF16),
            pltpu.VMEM((WIDE, band), BF16),
            pltpu.VMEM((4 * WIDE, LANES), F32),
        ],
        name="spectrum",
    )(row, *scalars, trig, spec_re, spec_im)
    info, cosine, sine, cos_k, sin_k, cos_y, sin_y = pl.pallas_call(
        tables_kernel,
        grid=(STEPS,),
        in_specs=[
            SCALARS,
            SCALARS,
            SCALARS,
            pl.BlockSpec((48, CHUNK), lambda n: (0, n)),
            pl.BlockSpec(memory_space=pl.ANY),
        ],
        out_specs=[WHOLE] + [col_block] * 6,
        out_shape=[jax.ShapeDtypeStruct((1, 8, LANES), F32)] + [table] * 6,
        cost_estimate=pl.CostEstimate(flops=18 * band * band, bytes_accessed=12 * band * band, transcendentals=0),
        name="tables",
    )(*scalars, trig, column_parts)
    all_info = gather_info(info)
    columns = exchange(column_parts.reshape(512, 8, LANES), everyone).reshape(4096, LANES)
    adjoint_parts = pl.pallas_call(
        image_kernel,
        grid=(STEPS + 2,),
        in_specs=[
            SCALARS,
            WHOLE,
            WHOLE,
            pl.BlockSpec((rows, CHUNK), lambda n: (0, jnp.minimum(n, STEPS - 1))),
            pl.BlockSpec((band, CHUNK), lambda n: (0, jnp.minimum(n, STEPS - 1))),
            pl.BlockSpec((band, CHUNK), lambda n: (0, jnp.minimum(n, STEPS - 1))),
            pl.BlockSpec((WIDE, band), lambda n: (jnp.maximum(n - STEPS, 0), 0)),
            pl.BlockSpec((WIDE, band), lambda n: (jnp.maximum(n - STEPS, 0), 0)),
        ],
        out_specs=pl.BlockSpec((16, 16, 8, LANES), lambda n: (0, jnp.maximum(n - STEPS, 0), 0, 0)),
        out_shape=parts,
        scratch_shapes=[
            pltpu.VMEM((512, band), BF16),
            pltpu.VMEM((STEPS, 512, CHUNK), BF16),
            pltpu.VMEM((4 * WIDE, LANES), F32),
        ],
        name="image",
    )(src, all_info, columns, target, cos_k, sin_k, cosine, sine)
    adjoint = exchange(adjoint_parts.reshape(512, 8, LANES), everyone).reshape(4096, LANES)
    gradient = pl.pallas_call(
        gradient_kernel,
        grid=(STEPS,),
        in_specs=[SCALARS, SCALARS, WHOLE, WHOLE, col_block, col_block],
        out_specs=WHOLE,
        out_shape=jax.ShapeDtypeStruct((16, 32, LANES), BF16),
        scratch_shapes=[
            pltpu.VMEM((512, band), BF16),
            pltpu.VMEM((4096, LANES), F32),
            pltpu.VMEM((32, LANES), F32),
        ],
        name="gradient",
    )(row * rows + 2 * src, src, all_info, adjoint, cos_y, sin_y)
    gradient = exchange(gradient, "src").reshape(512, LANES)
    out = jax.ShapeDtypeStruct((rows, band), F32)
    return tuple(
        pl.pallas_call(
            unpack_kernel, out_shape=[out, out], scratch_shapes=[pltpu.VMEM((512, LANES), F32)], name="unpack"
        )(gradient)
    )


def solution(mesh):
    return jax.shard_map(
        compute,
        mesh=mesh,
        in_specs=(P("row", None), P("row", None), P("row", None), P("src"), P("src"), P("src")),
        out_specs=(P("row", None), P("row", None)),
        check_vma=False,
    )
```

```python
import math

import jax
import jax.numpy as jnp
from jax import lax
from jax.experimental import pallas as pl
from jax.experimental.pallas import tpu as pltpu
from jax.sharding import PartitionSpec as P


RAD = 128
F32 = jnp.float32
BF16 = jnp.bfloat16
CHUNK = 256
WIDE = 512
LANES = 128
STEPS = 4

WHOLE = pl.BlockSpec(memory_space=pltpu.VMEM)
SCALARS = pl.BlockSpec(memory_space=pltpu.SMEM)


def trig_rows(band):
    index = jnp.arange(24, dtype=jnp.int32)
    rows = jnp.where(index < 8, index, 128 * (index - 8))
    rows = jnp.where(index < 16, rows, jnp.where(index < 20, 8 * (index - 16), 32 * (index - 20)))
    phase = rows[:, None] * jnp.arange(band, dtype=jnp.int32)[None, :]
    both = jnp.concatenate([phase, phase + (band - band // 4)], axis=0) % band
    return jnp.cos(both.astype(F32) * (2.0 * math.pi / band))


def rotate(one, other):
    return one[0] * other[0] - one[1] * other[1], one[1] * other[0] + one[0] * other[1]


def pick(trig, first, count=1):
    return trig[first : first + count, :], trig[24 + first : 24 + first + count, :]


def base_rows(trig, scale):
    fine = tuple(part * scale for part in pick(trig, 0, 8))
    blocks = [rotate(pick(trig, 16 + b), fine) for b in range(4)]
    return tuple(jnp.concatenate([block[i] for block in blocks], axis=0) for i in range(2))


def info_tile(w_ref, cr_ref, cc_ref):
    shape = (8, LANES)
    sublane = lax.broadcasted_iota(jnp.int32, shape, 0)
    lane = lax.broadcasted_iota(jnp.int32, shape, 1)
    tile = jnp.zeros(shape, F32)
    for p in range(8):
        centre = jnp.where(lane == 1, cr_ref[p].astype(F32), cc_ref[p].astype(F32))
        tile = jnp.where(sublane == p, jnp.where(lane == 0, jnp.sqrt(jnp.full(shape, w_ref[p], F32)), centre), tile)
    return tile


def dot_nt(left, right):
    return lax.dot_general(left, right, (((1,), (1,)), ((), ())), preferred_element_type=F32)


def dot_nn(left, right):
    return jnp.dot(left, right, preferred_element_type=F32)


def spectrum_kernel(row_ref, w_ref, cr_ref, cc_ref, trig_ref, re_ref, im_ref, out_ref, lhs_ref, cos_ref, sin_ref, flat_ref):
    step = pl.program_id(0)
    rows, band = re_ref.shape

    @pl.when(step == 0)
    def _():
        spec_re = re_ref[...].astype(F32)
        spec_im = im_ref[...].astype(F32)
        info = info_tile(w_ref, cr_ref, cc_ref)
        centre_row, centre_col = info[:, 1:2], info[:, 2:3]
        col_gap = lax.broadcasted_iota(jnp.int32, (8, band), 1).astype(F32) - centre_col
        col_gap = col_gap * col_gap
        first = (row_ref[0] * rows).astype(F32)
        for k in range(rows):
            row_gap = first + float(k) - centre_row
            keep = row_gap * row_gap + col_gap <= float(RAD * RAD)
            part_re = jnp.where(keep, spec_re[k : k + 1, :], 0.0)
            part_im = jnp.where(keep, spec_im[k : k + 1, :], 0.0)
            place = slice(16 * k, 16 * k + 16)
            lhs_ref[place, :band] = jnp.concatenate([part_re, part_im], axis=0).astype(BF16)
            lhs_ref[place, band:] = jnp.concatenate([-part_im, part_re], axis=0).astype(BF16)

    base = base_rows(trig_ref, 1.0 / math.sqrt(band))
    for a in range(4):
        coarse = tuple(trig_ref[pl.ds(first + 4 * step + a, 1), :] for first in (8, 32))
        for d in range(4):
            cos, sin = rotate(rotate(coarse, pick(trig_ref, 20 + d)), base)
            place = slice(128 * a + 32 * d, 128 * a + 32 * d + 32)
            cos_ref[place, :] = cos.astype(BF16)
            sin_ref[place, :] = sin.astype(BF16)
    product = dot_nt(cos_ref[...], lhs_ref[:, :band]) + dot_nt(sin_ref[...], lhs_ref[:, band:])
    point = lax.broadcasted_iota(jnp.int32, (8, LANES), 1) % 8
    root = jnp.zeros((8, LANES), F32)
    for p in range(8):
        root = jnp.where(point == p, w_ref[p], root)
    root = jnp.sqrt(root)[0:1, :]
    for t in range(4):
        flat_ref[pl.ds(t, WIDE, stride=4), :] = product[:, t * LANES : (t + 1) * LANES] * root
    low_row = lax.broadcasted_iota(jnp.int32, (8, LANES), 0) < 4
    low_lane = lax.broadcasted_iota(jnp.int32, (8, LANES), 1) < 64
    stay = low_row == low_lane
    for r in range(16):
        for s in range(16):
            first_row = 8 * (16 * r + s)
            tile = flat_ref[first_row : first_row + 8, :]
            moved = pltpu.roll(pltpu.roll(tile, 4, 0), 64, 1)
            out_ref[s, r] = jnp.where(stay, tile, moved).astype(BF16)


def tables_kernel(
    w_ref, cr_ref, cc_ref, trig_ref, _, info_ref, cos_ref, sin_ref, cos_k_ref, sin_k_ref, cos_y_ref, sin_y_ref
):
    @pl.when(pl.program_id(0) == 0)
    def _():
        info_ref[0] = info_tile(w_ref, cr_ref, cc_ref)

    base_c, base_s = base_rows(trig_ref, 1.0 / math.sqrt(4 * trig_ref.shape[1]))
    turns = [rotate(pick(trig_ref, 8 + a), pick(trig_ref, 20 + d)) for a in range(8) for d in range(4)]
    turn_c, turn_s = (jnp.concatenate([turn[i] for turn in turns], axis=0) for i in range(2))
    for r in range(32):
        cos, sin = rotate(turns[r], (base_c, base_s))
        cos_ref[32 * r : 32 * r + 32, :] = cos.astype(BF16)
        sin_ref[32 * r : 32 * r + 32, :] = sin.astype(BF16)
    for j in range(4):
        order = [j + 8 * (i % 4) + 4 * (i // 4) for i in range(8)]
        near_c = jnp.concatenate([base_c[f : f + 1, :] for f in order], axis=0)
        near_s = jnp.concatenate([base_s[f : f + 1, :] for f in order], axis=0)
        for r in range(0, 32, 2):
            cs, ss = [], []
            for turn in (r, r + 1):
                c, s = turn_c[turn : turn + 1, :], turn_s[turn : turn + 1, :]
                cs.append(c * near_c - s * near_s)
                ss.append(s * near_c + c * near_s)
            place = slice(256 * j + 8 * r, 256 * j + 8 * r + 16)
            cos_k_ref[place, :] = jnp.concatenate(cs, axis=0).astype(BF16)
            sin_k_ref[place, :] = jnp.concatenate(ss, axis=0).astype(BF16)
    for f in range(32):
        c, s = base_c[f : f + 1, :], base_s[f : f + 1, :]
        first = 512 * (f % 2) + 32 * (f // 2)
        cos_y_ref[first : first + 32, :] = (c * turn_c - s * turn_s).astype(BF16)
        sin_y_ref[first : first + 32, :] = (s * turn_c + c * turn_s).astype(BF16)


def image_kernel(
    src_ref,
    info_ref,
    in_ref,
    target_ref,
    cos_k_ref,
    sin_k_ref,
    cos_ref,
    sin_ref,
    out_ref,
    info_out_ref,
    lhs_ref,
    grad_ref,
    flat_ref,
):
    step = pl.program_id(0)

    @pl.when(step == 0)
    def _():
        info_out_ref[...] = info_ref[...]
        for s in range(16):
            turned = in_ref[256 * s : 256 * s + 256, :].T
            for y in range(2):
                for j in range(4):
                    lhs_ref[32 * s + 16 * y : 32 * s + 16 * y + 16, 256 * j : 256 * j + 256] = turned[
                        64 * y + 16 * j : 64 * y + 16 * j + 16
                    ]

    @pl.when(step < STEPS)
    def _():
        by_cos = dot_nn(lhs_ref[...], cos_k_ref[...])
        by_sin = dot_nn(lhs_ref[...], sin_k_ref[...])

        def field(s, y):
            at = 32 * s + 16 * y
            re = by_cos[at : at + 8] - by_sin[at + 8 : at + 16]
            im = by_sin[at : at + 8] + by_cos[at + 8 : at + 16]
            return re, im

        for y in range(2):
            power = jnp.zeros((8, CHUNK), F32)
            for s in range(16):
                re, im = field(s, y)
                power += re * re + im * im
            intensity = jnp.sum(power, axis=0, keepdims=True) * (1.0 / 128.0)
            mismatch = intensity - target_ref[pl.ds(2 * src_ref[0] + y, 1), :]
            factor = 2.0 * mismatch
            for s in range(0, 16, 2):
                grads_re, grads_im = [], []
                for one in (s, s + 1):
                    re, im = field(one, y)
                    grads_re.append(factor * re)
                    grads_im.append(factor * im)
                at = 256 * y + 8 * s
                grad_ref[step, at : at + 16, :] = jnp.concatenate(grads_re, axis=0).astype(BF16)
                grad_ref[step, at + 128 : at + 144, :] = jnp.concatenate(grads_im, axis=0).astype(BF16)

    @pl.when(step >= STEPS)
    def _():
        by_cos = jnp.zeros((WIDE, 512), F32)
        by_sin = jnp.zeros((WIDE, 512), F32)
        for n in range(STEPS):
            cols = slice(n * CHUNK, (n + 1) * CHUNK)
            by_cos += dot_nt(cos_ref[:, cols], grad_ref[n])
            by_sin += dot_nt(sin_ref[:, cols], grad_ref[n])
        for y in range(2):
            re, im = slice(256 * y, 256 * y + 128), slice(256 * y + 128, 256 * y + 256)
            flat_ref[pl.ds(2 * y, WIDE, stride=4), :] = by_cos[:, re] + by_sin[:, im]
            flat_ref[pl.ds(2 * y + 1, WIDE, stride=4), :] = by_cos[:, im] - by_sin[:, re]
        for r in range(16):
            for s in range(16):
                first_row = 8 * (16 * r + s)
                out_ref[s, r] = flat_ref[first_row : first_row + 8, :].astype(BF16)


def gradient_kernel(place_ref, src_ref, info_ref, in_ref, cos_ref, sin_ref, out_ref, lhs_ref, flat_ref, sums_ref):
    step = pl.program_id(0)

    @pl.when(step == 0)
    def _():
        for first in range(0, 4096, 512):
            flat_ref[first : first + 512, :] = in_ref[first : first + 512, :].astype(F32)
        for k in range(2):
            for y in range(2):
                for c in range(2):
                    part = flat_ref[pl.ds(4 * k + 2 * y + c, 512, stride=8), :]
                    lhs_ref[128 * (2 * c + k) : 128 * (2 * c + k) + 128, 512 * y : 512 * y + 512] = part.T.astype(BF16)

    by_cos = dot_nn(lhs_ref[...], cos_ref[...])
    by_sin = dot_nn(lhs_ref[...], sin_ref[...])
    info = jnp.concatenate([info_ref[jnp.bitwise_xor(src_ref[0], s)] for s in range(16)], axis=0)
    root, centre_row, centre_col = info[:, 0:1], info[:, 1:2], info[:, 2:3]
    first_col = (step * CHUNK).astype(F32)
    col_gap = lax.broadcasted_iota(jnp.int32, (LANES, CHUNK), 1).astype(F32) + (first_col - centre_col)
    col_gap = col_gap * col_gap
    for k in range(2):
        row_gap = (place_ref[0] + k).astype(F32) - centre_row
        keep = row_gap * row_gap + col_gap <= float(RAD * RAD)
        factor = jnp.where(keep, root, 0.0)
        re, im = slice(128 * k, 128 * k + 128), slice(256 + 128 * k, 256 + 128 * k + 128)
        terms = (by_cos[re] + by_sin[im], by_cos[im] - by_sin[re])
        for c in range(2):
            total = jnp.sum(factor * terms[c], axis=0, keepdims=True)
            for side in range(2):
                sums_ref[pl.ds(16 * k + 8 * c + 2 * step + side, 1), :] = total[:, side * LANES : (side + 1) * LANES]

    @pl.when(step == STEPS - 1)
    def _():
        for i in range(16):
            out_ref[i] = sums_ref[...].astype(BF16)


def unpack_kernel(in_ref, re_ref, im_ref, flat_ref):
    flat_ref[...] = in_ref[...].astype(F32)
    for c, ref in enumerate((re_ref, im_ref)):
        for tile in range(8):
            ref[:, tile * LANES : (tile + 1) * LANES] = flat_ref[pl.ds(8 * c + tile, 32, stride=16), :]


def exchange(value, axis):
    return lax.all_to_all(value, axis, split_axis=0, concat_axis=0, tiled=True)


def gather_info(info, bits):
    for bit in bits:
        info = jnp.concatenate([info, lax.ppermute(info, "src", [(i, i ^ bit) for i in range(16)])], axis=0)
    return info


def compute(spec_re, spec_im, target, weights, cent_row, cent_col):
    rows, band = spec_re.shape
    everyone = ("src", "row")
    row = lax.axis_index("row").astype(jnp.int32).reshape(1)
    src = lax.axis_index("src").astype(jnp.int32).reshape(1)
    trig = trig_rows(band)
    table = jax.ShapeDtypeStruct((band, band), BF16)
    parts = jax.ShapeDtypeStruct((16, 32, 8, LANES), BF16)
    col_block = pl.BlockSpec((band, CHUNK), lambda n: (0, n))
    scalars = (weights, cent_row, cent_col)

    column_parts = pl.pallas_call(
        spectrum_kernel,
        grid=(2,),
        in_specs=[SCALARS, SCALARS, SCALARS, SCALARS, WHOLE, WHOLE, WHOLE],
        out_specs=pl.BlockSpec((16, 16, 8, LANES), lambda n: (0, n, 0, 0)),
        out_shape=parts,
        scratch_shapes=[
            pltpu.VMEM((512, 2 * band), BF16),
            pltpu.VMEM((WIDE, band), BF16),
            pltpu.VMEM((WIDE, band), BF16),
            pltpu.VMEM((4 * WIDE, LANES), F32),
        ],
        name="spectrum",
    )(row, *scalars, trig, spec_re, spec_im)
    info, cosine, sine, cos_k, sin_k, cos_y, sin_y = pl.pallas_call(
        tables_kernel,
        grid=(STEPS,),
        in_specs=[
            SCALARS,
            SCALARS,
            SCALARS,
            pl.BlockSpec((48, CHUNK), lambda n: (0, n)),
            pl.BlockSpec(memory_space=pl.ANY),
        ],
        out_specs=[WHOLE] + [col_block] * 6,
        out_shape=[jax.ShapeDtypeStruct((1, 8, LANES), F32)] + [table] * 6,
        cost_estimate=pl.CostEstimate(flops=18 * band * band, bytes_accessed=12 * band * band, transcendentals=0),
        name="tables",
    )(*scalars, trig, column_parts)
    some_info = gather_info(info, (1, 2))
    columns = exchange(column_parts.reshape(512, 8, LANES), everyone).reshape(4096, LANES)
    adjoint_parts, some_info = pl.pallas_call(
        image_kernel,
        grid=(STEPS + 2,),
        in_specs=[
            SCALARS,
            WHOLE,
            WHOLE,
            pl.BlockSpec((rows, CHUNK), lambda n: (0, jnp.minimum(n, STEPS - 1))),
            pl.BlockSpec((band, CHUNK), lambda n: (0, jnp.minimum(n, STEPS - 1))),
            pl.BlockSpec((band, CHUNK), lambda n: (0, jnp.minimum(n, STEPS - 1))),
            pl.BlockSpec((WIDE, band), lambda n: (jnp.maximum(n - STEPS, 0), 0)),
            pl.BlockSpec((WIDE, band), lambda n: (jnp.maximum(n - STEPS, 0), 0)),
        ],
        out_specs=[pl.BlockSpec((16, 16, 8, LANES), lambda n: (0, jnp.maximum(n - STEPS, 0), 0, 0)), WHOLE],
        out_shape=[parts, jax.ShapeDtypeStruct((4, 8, LANES), F32)],
        scratch_shapes=[
            pltpu.VMEM((512, band), BF16),
            pltpu.VMEM((STEPS, 512, CHUNK), BF16),
            pltpu.VMEM((4 * WIDE, LANES), F32),
        ],
        name="image",
    )(src, some_info, columns, target, cos_k, sin_k, cosine, sine)
    adjoint = exchange(adjoint_parts.reshape(512, 8, LANES), everyone).reshape(4096, LANES)
    all_info = gather_info(some_info, (4, 8))
    gradient = pl.pallas_call(
        gradient_kernel,
        grid=(STEPS,),
        in_specs=[SCALARS, SCALARS, WHOLE, WHOLE, col_block, col_block],
        out_specs=WHOLE,
        out_shape=jax.ShapeDtypeStruct((16, 32, LANES), BF16),
        scratch_shapes=[
            pltpu.VMEM((512, band), BF16),
            pltpu.VMEM((4096, LANES), F32),
            pltpu.VMEM((32, LANES), F32),
        ],
        name="gradient",
    )(row * rows + 2 * src, src, all_info, adjoint, cos_y, sin_y)
    gradient = exchange(gradient, "src").reshape(512, LANES)
    out = jax.ShapeDtypeStruct((rows, band), F32)
    return tuple(
        pl.pallas_call(
            unpack_kernel, out_shape=[out, out], scratch_shapes=[pltpu.VMEM((512, LANES), F32)], name="unpack"
        )(gradient)
    )


def solution(mesh):
    return jax.shard_map(
        compute,
        mesh=mesh,
        in_specs=(P("row", None), P("row", None), P("row", None), P("src"), P("src"), P("src")),
        out_specs=(P("row", None), P("row", None)),
        check_vma=False,
    )
```

```python
import math

import jax
import jax.numpy as jnp
from jax import lax
from jax.experimental import pallas as pl
from jax.experimental.pallas import tpu as pltpu
from jax.sharding import PartitionSpec as P


RAD = 128
F32 = jnp.float32
BF16 = jnp.bfloat16
CHUNK = 256
WIDE = 512
LANES = 128
STEPS = 4

WHOLE = pl.BlockSpec(memory_space=pltpu.VMEM)
SCALARS = pl.BlockSpec(memory_space=pltpu.SMEM)


def trig_rows(band):
    index = jnp.arange(24, dtype=jnp.int32)
    rows = jnp.where(index < 8, index, 128 * (index - 8))
    rows = jnp.where(index < 16, rows, jnp.where(index < 20, 8 * (index - 16), 32 * (index - 20)))
    phase = rows[:, None] * jnp.arange(band, dtype=jnp.int32)[None, :]
    both = jnp.concatenate([phase, phase + (band - band // 4)], axis=0) % band
    return jnp.cos(both.astype(F32) * (2.0 * math.pi / band))


def rotate(one, other):
    return one[0] * other[0] - one[1] * other[1], one[1] * other[0] + one[0] * other[1]


def pick(trig, first, count=1):
    return trig[first : first + count, :], trig[24 + first : 24 + first + count, :]


def base_rows(trig, scale):
    fine = tuple(part * scale for part in pick(trig, 0, 8))
    blocks = [rotate(pick(trig, 16 + b), fine) for b in range(4)]
    return tuple(jnp.concatenate([block[i] for block in blocks], axis=0) for i in range(2))


def info_tile(w_ref, cr_ref, cc_ref):
    shape = (8, LANES)
    sublane = lax.broadcasted_iota(jnp.int32, shape, 0)
    lane = lax.broadcasted_iota(jnp.int32, shape, 1)
    tile = jnp.zeros(shape, F32)
    for p in range(8):
        centre = jnp.where(lane == 1, cr_ref[p].astype(F32), cc_ref[p].astype(F32))
        tile = jnp.where(sublane == p, jnp.where(lane == 0, jnp.sqrt(jnp.full(shape, w_ref[p], F32)), centre), tile)
    return tile


def dot_nt(left, right):
    return lax.dot_general(left, right, (((1,), (1,)), ((), ())), preferred_element_type=F32)


def dot_nn(left, right):
    return jnp.dot(left, right, preferred_element_type=F32)


def spectrum_kernel(row_ref, w_ref, cr_ref, cc_ref, trig_ref, re_ref, im_ref, out_ref, lhs_ref, table_ref, flat_ref):
    step = pl.program_id(0)
    rows, band = re_ref.shape

    @pl.when(step == 0)
    def _():
        spec_re = re_ref[...].astype(F32)
        spec_im = im_ref[...].astype(F32)
        info = info_tile(w_ref, cr_ref, cc_ref)
        centre_row, centre_col = info[:, 1:2], info[:, 2:3]
        col_gap = lax.broadcasted_iota(jnp.int32, (8, band), 1).astype(F32) - centre_col
        col_gap = col_gap * col_gap
        first = (row_ref[0] * rows).astype(F32)
        for k in range(rows):
            row_gap = first + float(k) - centre_row
            keep = row_gap * row_gap + col_gap <= float(RAD * RAD)
            part_re = jnp.where(keep, spec_re[k : k + 1, :], 0.0)
            part_im = jnp.where(keep, spec_im[k : k + 1, :], 0.0)
            place = slice(16 * k, 16 * k + 16)
            lhs_ref[place, :band] = jnp.concatenate([part_re, part_im], axis=0).astype(BF16)
            lhs_ref[place, band:] = jnp.concatenate([-part_im, part_re], axis=0).astype(BF16)

    base = base_rows(trig_ref, 1.0 / math.sqrt(band))
    for a in range(4):
        coarse = tuple(trig_ref[pl.ds(first + 4 * step + a, 1), :] for first in (8, 32))
        for d in range(4):
            cos, sin = rotate(rotate(coarse, pick(trig_ref, 20 + d)), base)
            place = slice(128 * a + 32 * d, 128 * a + 32 * d + 32)
            table_ref[place, :band] = cos.astype(BF16)
            table_ref[place, band:] = sin.astype(BF16)
    product = dot_nt(table_ref[...], lhs_ref[...])
    point = lax.broadcasted_iota(jnp.int32, (8, LANES), 1) % 8
    root = jnp.zeros((8, LANES), F32)
    for p in range(8):
        root = jnp.where(point == p, w_ref[p], root)
    root = jnp.sqrt(root)[0:1, :]
    for t in range(4):
        flat_ref[pl.ds(t, WIDE, stride=4), :] = product[:, t * LANES : (t + 1) * LANES] * root
    low_row = lax.broadcasted_iota(jnp.int32, (8, LANES), 0) < 4
    low_lane = lax.broadcasted_iota(jnp.int32, (8, LANES), 1) < 64
    stay = low_row == low_lane
    for r in range(16):
        for s in range(16):
            first_row = 8 * (16 * r + s)
            tile = flat_ref[first_row : first_row + 8, :]
            moved = pltpu.roll(pltpu.roll(tile, 4, 0), 64, 1)
            out_ref[s, r] = jnp.where(stay, tile, moved).astype(BF16)


def tables_kernel(
    w_ref, cr_ref, cc_ref, trig_ref, _, info_ref, cos_ref, sin_ref, cos_k_ref, sin_k_ref, cos_y_ref, sin_y_ref
):
    @pl.when(pl.program_id(0) == 0)
    def _():
        info_ref[0] = info_tile(w_ref, cr_ref, cc_ref)

    base_c, base_s = base_rows(trig_ref, 1.0 / math.sqrt(4 * trig_ref.shape[1]))
    turns = [rotate(pick(trig_ref, 8 + a), pick(trig_ref, 20 + d)) for a in range(8) for d in range(4)]
    turn_c, turn_s = (jnp.concatenate([turn[i] for turn in turns], axis=0) for i in range(2))
    for r in range(32):
        cos, sin = rotate(turns[r], (base_c, base_s))
        cos_ref[32 * r : 32 * r + 32, :] = cos.astype(BF16)
        sin_ref[32 * r : 32 * r + 32, :] = sin.astype(BF16)
    for j in range(4):
        order = [j + 8 * (i % 4) + 4 * (i // 4) for i in range(8)]
        near_c = jnp.concatenate([base_c[f : f + 1, :] for f in order], axis=0)
        near_s = jnp.concatenate([base_s[f : f + 1, :] for f in order], axis=0)
        for r in range(0, 32, 2):
            cs, ss = [], []
            for turn in (r, r + 1):
                c, s = turn_c[turn : turn + 1, :], turn_s[turn : turn + 1, :]
                cs.append(c * near_c - s * near_s)
                ss.append(s * near_c + c * near_s)
            place = slice(256 * j + 8 * r, 256 * j + 8 * r + 16)
            cos_k_ref[place, :] = jnp.concatenate(cs, axis=0).astype(BF16)
            sin_k_ref[place, :] = jnp.concatenate(ss, axis=0).astype(BF16)
    for f in range(32):
        c, s = base_c[f : f + 1, :], base_s[f : f + 1, :]
        first = 512 * (f % 2) + 32 * (f // 2)
        cos_y_ref[first : first + 32, :] = (c * turn_c - s * turn_s).astype(BF16)
        sin_y_ref[first : first + 32, :] = (s * turn_c + c * turn_s).astype(BF16)


def image_kernel(
    src_ref,
    info_ref,
    in_ref,
    target_ref,
    cos_k_ref,
    sin_k_ref,
    cos_ref,
    sin_ref,
    out_ref,
    info_out_ref,
    lhs_ref,
    grad_ref,
    flat_ref,
):
    step = pl.program_id(0)

    @pl.when(step == 0)
    def _():
        info_out_ref[...] = info_ref[...]
        for s in range(16):
            turned = in_ref[256 * s : 256 * s + 256, :].T
            for y in range(2):
                for j in range(4):
                    lhs_ref[32 * s + 16 * y : 32 * s + 16 * y + 16, 256 * j : 256 * j + 256] = turned[
                        64 * y + 16 * j : 64 * y + 16 * j + 16
                    ]

    @pl.when(step < STEPS)
    def _():
        by_cos = dot_nn(lhs_ref[...], cos_k_ref[...])
        by_sin = dot_nn(lhs_ref[...], sin_k_ref[...])

        cols = pl.ds(pl.multiple_of(step * CHUNK, CHUNK), CHUNK)

        def field(s, y):
            at = 32 * s + 16 * y
            re = by_cos[at : at + 8] - by_sin[at + 8 : at + 16]
            im = by_sin[at : at + 8] + by_cos[at + 8 : at + 16]
            return re, im

        for y in range(2):
            power = jnp.zeros((8, CHUNK), F32)
            for s in range(16):
                re, im = field(s, y)
                power += re * re + im * im
            intensity = jnp.sum(power, axis=0, keepdims=True) * (1.0 / 128.0)
            mismatch = intensity - target_ref[pl.ds(2 * src_ref[0] + y, 1), :]
            factor = 2.0 * mismatch
            for s in range(0, 16, 2):
                grads_re, grads_im = [], []
                for one in (s, s + 1):
                    re, im = field(one, y)
                    grads_re.append(factor * re)
                    grads_im.append(factor * im)
                at = 256 * y + 8 * s
                grad_ref[at : at + 16, cols] = jnp.concatenate(grads_re, axis=0).astype(BF16)
                grad_ref[at + 128 : at + 144, cols] = jnp.concatenate(grads_im, axis=0).astype(BF16)

    @pl.when(step >= STEPS)
    def _():
        by_cos = dot_nt(cos_ref[...], grad_ref[...])
        by_sin = dot_nt(sin_ref[...], grad_ref[...])
        for y in range(2):
            re, im = slice(256 * y, 256 * y + 128), slice(256 * y + 128, 256 * y + 256)
            flat_ref[pl.ds(2 * y, WIDE, stride=4), :] = by_cos[:, re] + by_sin[:, im]
            flat_ref[pl.ds(2 * y + 1, WIDE, stride=4), :] = by_cos[:, im] - by_sin[:, re]
        for r in range(16):
            for s in range(16):
                first_row = 8 * (16 * r + s)
                out_ref[s, r] = flat_ref[first_row : first_row + 8, :].astype(BF16)


def gradient_kernel(place_ref, src_ref, info_ref, in_ref, cos_ref, sin_ref, out_ref, lhs_ref, flat_ref, sums_ref):
    step = pl.program_id(0)

    @pl.when(step == 0)
    def _():
        for first in range(0, 4096, 512):
            flat_ref[first : first + 512, :] = in_ref[first : first + 512, :].astype(F32)
        for k in range(2):
            for y in range(2):
                for c in range(2):
                    part = flat_ref[pl.ds(4 * k + 2 * y + c, 512, stride=8), :]
                    lhs_ref[128 * (2 * c + k) : 128 * (2 * c + k) + 128, 512 * y : 512 * y + 512] = part.astype(BF16).T

    by_cos = dot_nn(lhs_ref[...], cos_ref[...])
    by_sin = dot_nn(lhs_ref[...], sin_ref[...])
    gaps = [jnp.bitwise_xor(src_ref[0], s) for s in range(16)]
    info = jnp.concatenate([info_ref[gap // 2 + 8 * (gap % 2)] for gap in gaps], axis=0)
    root, centre_row, centre_col = info[:, 0:1], info[:, 1:2], info[:, 2:3]
    first_col = (step * CHUNK).astype(F32)
    col_gap = lax.broadcasted_iota(jnp.int32, (LANES, CHUNK), 1).astype(F32) + (first_col - centre_col)
    col_gap = col_gap * col_gap
    for k in range(2):
        row_gap = (place_ref[0] + k).astype(F32) - centre_row
        keep = row_gap * row_gap + col_gap <= float(RAD * RAD)
        factor = jnp.where(keep, root, 0.0)
        re, im = slice(128 * k, 128 * k + 128), slice(256 + 128 * k, 256 + 128 * k + 128)
        terms = (by_cos[re] + by_sin[im], by_cos[im] - by_sin[re])
        for c in range(2):
            total = jnp.sum(factor * terms[c], axis=0, keepdims=True)
            for side in range(2):
                sums_ref[pl.ds(16 * k + 8 * c + 2 * step + side, 1), :] = total[:, side * LANES : (side + 1) * LANES]

    @pl.when(step == STEPS - 1)
    def _():
        for i in range(16):
            out_ref[i] = sums_ref[...].astype(BF16)


def unpack_kernel(in_ref, re_ref, im_ref, flat_ref):
    flat_ref[...] = in_ref[...].astype(F32)
    for c, ref in enumerate((re_ref, im_ref)):
        for tile in range(8):
            ref[:, tile * LANES : (tile + 1) * LANES] = flat_ref[pl.ds(8 * c + tile, 32, stride=16), :]


def exchange(value, axis):
    return lax.all_to_all(value, axis, split_axis=0, concat_axis=0, tiled=True)


def gather_info(info, bits):
    for bit in bits:
        info = jnp.concatenate([info, lax.ppermute(info, "src", [(i, i ^ bit) for i in range(16)])], axis=0)
    return info


def compute(spec_re, spec_im, target, weights, cent_row, cent_col):
    rows, band = spec_re.shape
    everyone = ("src", "row")
    row = lax.axis_index("row").astype(jnp.int32).reshape(1)
    src = lax.axis_index("src").astype(jnp.int32).reshape(1)
    trig = trig_rows(band)
    table = jax.ShapeDtypeStruct((band, band), BF16)
    parts = jax.ShapeDtypeStruct((16, 32, 8, LANES), BF16)
    col_block = pl.BlockSpec((band, CHUNK), lambda n: (0, n))
    scalars = (weights, cent_row, cent_col)

    column_parts = pl.pallas_call(
        spectrum_kernel,
        grid=(2,),
        in_specs=[SCALARS, SCALARS, SCALARS, SCALARS, WHOLE, WHOLE, WHOLE],
        out_specs=pl.BlockSpec((16, 16, 8, LANES), lambda n: (0, n, 0, 0)),
        out_shape=parts,
        scratch_shapes=[
            pltpu.VMEM((512, 2 * band), BF16),
            pltpu.VMEM((WIDE, 2 * band), BF16),
            pltpu.VMEM((4 * WIDE, LANES), F32),
        ],
        name="spectrum",
    )(row, *scalars, trig, spec_re, spec_im)
    info, cosine, sine, cos_k, sin_k, cos_y, sin_y = pl.pallas_call(
        tables_kernel,
        grid=(STEPS,),
        in_specs=[
            SCALARS,
            SCALARS,
            SCALARS,
            pl.BlockSpec((48, CHUNK), lambda n: (0, n)),
            pl.BlockSpec(memory_space=pl.ANY),
        ],
        out_specs=[WHOLE] + [col_block] * 6,
        out_shape=[jax.ShapeDtypeStruct((1, 8, LANES), F32)] + [table] * 6,
        cost_estimate=pl.CostEstimate(flops=18 * band * band, bytes_accessed=12 * band * band, transcendentals=0),
        name="tables",
    )(*scalars, trig, column_parts)
    some_info = gather_info(info, (2, 4))
    columns = exchange(column_parts.reshape(512, 8, LANES), everyone).reshape(4096, LANES)
    adjoint_parts, some_info = pl.pallas_call(
        image_kernel,
        grid=(STEPS + 2,),
        in_specs=[
            SCALARS,
            WHOLE,
            WHOLE,
            pl.BlockSpec((rows, CHUNK), lambda n: (0, jnp.minimum(n, STEPS - 1))),
            pl.BlockSpec((band, CHUNK), lambda n: (0, jnp.minimum(n, STEPS - 1))),
            pl.BlockSpec((band, CHUNK), lambda n: (0, jnp.minimum(n, STEPS - 1))),
            pl.BlockSpec((WIDE, band), lambda n: (jnp.maximum(n - STEPS, 0), 0)),
            pl.BlockSpec((WIDE, band), lambda n: (jnp.maximum(n - STEPS, 0), 0)),
        ],
        out_specs=[pl.BlockSpec((16, 16, 8, LANES), lambda n: (0, jnp.maximum(n - STEPS, 0), 0, 0)), WHOLE],
        out_shape=[parts, jax.ShapeDtypeStruct((4, 8, LANES), F32)],
        scratch_shapes=[
            pltpu.VMEM((512, band), BF16),
            pltpu.VMEM((512, band), BF16),
            pltpu.VMEM((4 * WIDE, LANES), F32),
        ],
        name="image",
    )(src, some_info, columns, target, cos_k, sin_k, cosine, sine)
    adjoint = exchange(adjoint_parts.reshape(512, 8, LANES), everyone).reshape(4096, LANES)
    all_info = gather_info(some_info, (8, 1))
    gradient = pl.pallas_call(
        gradient_kernel,
        grid=(STEPS,),
        in_specs=[SCALARS, SCALARS, WHOLE, WHOLE, col_block, col_block],
        out_specs=WHOLE,
        out_shape=jax.ShapeDtypeStruct((16, 32, LANES), BF16),
        scratch_shapes=[
            pltpu.VMEM((512, band), BF16),
            pltpu.VMEM((4096, LANES), F32),
            pltpu.VMEM((32, LANES), F32),
        ],
        name="gradient",
    )(row * rows + 2 * src, src, all_info, adjoint, cos_y, sin_y)
    gradient = exchange(gradient, "src").reshape(512, LANES)
    out = jax.ShapeDtypeStruct((rows, band), F32)
    return tuple(
        pl.pallas_call(
            unpack_kernel, out_shape=[out, out], scratch_shapes=[pltpu.VMEM((512, LANES), F32)], name="unpack"
        )(gradient)
    )


def solution(mesh):
    return jax.shard_map(
        compute,
        mesh=mesh,
        in_specs=(P("row", None), P("row", None), P("row", None), P("src"), P("src"), P("src")),
        out_specs=(P("row", None), P("row", None)),
        check_vma=False,
    )
```

```python
import math

import jax
import jax.numpy as jnp
from jax import lax
from jax.experimental import pallas as pl
from jax.experimental.pallas import tpu as pltpu
from jax.sharding import PartitionSpec as P


RAD = 128
F32 = jnp.float32
BF16 = jnp.bfloat16
CHUNK = 256
WIDE = 512
LANES = 128
STEPS = 4

WHOLE = pl.BlockSpec(memory_space=pltpu.VMEM)
SCALARS = pl.BlockSpec(memory_space=pltpu.SMEM)


def trig_rows(band):
    index = jnp.arange(24, dtype=jnp.int32)
    rows = jnp.where(index < 8, index, 128 * (index - 8))
    rows = jnp.where(index < 16, rows, jnp.where(index < 20, 8 * (index - 16), 32 * (index - 20)))
    phase = rows[:, None] * jnp.arange(band, dtype=jnp.int32)[None, :]
    both = jnp.concatenate([phase, phase + (band - band // 4)], axis=0) % band
    return jnp.cos(both.astype(F32) * (2.0 * math.pi / band))


def rotate(one, other):
    return one[0] * other[0] - one[1] * other[1], one[1] * other[0] + one[0] * other[1]


def pick(trig, first, count=1):
    return trig[first : first + count, :], trig[24 + first : 24 + first + count, :]


def base_rows(trig, scale):
    fine = tuple(part * scale for part in pick(trig, 0, 8))
    blocks = [rotate(pick(trig, 16 + b), fine) for b in range(4)]
    return tuple(jnp.concatenate([block[i] for block in blocks], axis=0) for i in range(2))


def info_tile(w_ref, cr_ref, cc_ref):
    shape = (8, LANES)
    sublane = lax.broadcasted_iota(jnp.int32, shape, 0)
    lane = lax.broadcasted_iota(jnp.int32, shape, 1)
    tile = jnp.zeros(shape, F32)
    for p in range(8):
        centre = jnp.where(lane == 1, cr_ref[p].astype(F32), cc_ref[p].astype(F32))
        tile = jnp.where(sublane == p, jnp.where(lane == 0, jnp.sqrt(jnp.full(shape, w_ref[p], F32)), centre), tile)
    return tile


def dot_nt(left, right):
    return lax.dot_general(left, right, (((1,), (1,)), ((), ())), preferred_element_type=F32)


def dot_nn(left, right):
    return jnp.dot(left, right, preferred_element_type=F32)


def spectrum_kernel(row_ref, w_ref, cr_ref, cc_ref, trig_ref, re_ref, im_ref, out_ref, info_ref, lhs_ref, table_ref, flat_ref):
    step = pl.program_id(0)
    rows, band = re_ref.shape

    @pl.when(step == 0)
    def _():
        spec_re = re_ref[...].astype(F32)
        spec_im = im_ref[...].astype(F32)
        info = info_tile(w_ref, cr_ref, cc_ref)
        info_ref[0] = info
        centre_row, centre_col = info[:, 1:2], info[:, 2:3]
        col_gap = lax.broadcasted_iota(jnp.int32, (8, band), 1).astype(F32) - centre_col
        col_gap = col_gap * col_gap
        first = (row_ref[0] * rows).astype(F32)
        for k in range(rows):
            row_gap = first + float(k) - centre_row
            keep = row_gap * row_gap + col_gap <= float(RAD * RAD)
            part_re = jnp.where(keep, spec_re[k : k + 1, :], 0.0)
            part_im = jnp.where(keep, spec_im[k : k + 1, :], 0.0)
            place = slice(16 * k, 16 * k + 16)
            lhs_ref[place, :band] = jnp.concatenate([part_re, part_im], axis=0).astype(BF16)
            lhs_ref[place, band:] = jnp.concatenate([-part_im, part_re], axis=0).astype(BF16)

    base = base_rows(trig_ref, 1.0 / math.sqrt(band))
    for a in range(4):
        coarse = tuple(trig_ref[pl.ds(first + 4 * step + a, 1), :] for first in (8, 32))
        for d in range(4):
            cos, sin = rotate(rotate(coarse, pick(trig_ref, 20 + d)), base)
            place = slice(128 * a + 32 * d, 128 * a + 32 * d + 32)
            table_ref[place, :band] = cos.astype(BF16)
            table_ref[place, band:] = sin.astype(BF16)
    product = dot_nt(table_ref[...], lhs_ref[...])
    point = lax.broadcasted_iota(jnp.int32, (8, LANES), 1) % 8
    root = jnp.zeros((8, LANES), F32)
    for p in range(8):
        root = jnp.where(point == p, w_ref[p], root)
    root = jnp.sqrt(root)[0:1, :]
    for t in range(4):
        flat_ref[pl.ds(t, WIDE, stride=4), :] = product[:, t * LANES : (t + 1) * LANES] * root
    low_row = lax.broadcasted_iota(jnp.int32, (8, LANES), 0) < 4
    low_lane = lax.broadcasted_iota(jnp.int32, (8, LANES), 1) < 64
    stay = low_row == low_lane
    for r in range(16):
        for s in range(16):
            first_row = 8 * (16 * r + s)
            tile = flat_ref[first_row : first_row + 8, :]
            moved = pltpu.roll(pltpu.roll(tile, 4, 0), 64, 1)
            out_ref[s, r] = jnp.where(stay, tile, moved).astype(BF16)


def tables_kernel(
    trig_ref, _, cos_ref, sin_ref, cos_k_ref, sin_k_ref, cos_y_ref, sin_y_ref
):
    base_c, base_s = base_rows(trig_ref, 1.0 / math.sqrt(4 * trig_ref.shape[1]))
    turns = [rotate(pick(trig_ref, 8 + a), pick(trig_ref, 20 + d)) for a in range(8) for d in range(4)]
    turn_c, turn_s = (jnp.concatenate([turn[i] for turn in turns], axis=0) for i in range(2))
    for r in range(32):
        cos, sin = rotate(turns[r], (base_c, base_s))
        cos_ref[32 * r : 32 * r + 32, :] = cos.astype(BF16)
        sin_ref[32 * r : 32 * r + 32, :] = sin.astype(BF16)
    for j in range(4):
        order = [j + 8 * (i % 4) + 4 * (i // 4) for i in range(8)]
        near_c = jnp.concatenate([base_c[f : f + 1, :] for f in order], axis=0)
        near_s = jnp.concatenate([base_s[f : f + 1, :] for f in order], axis=0)
        for r in range(0, 32, 2):
            cs, ss = [], []
            for turn in (r, r + 1):
                c, s = turn_c[turn : turn + 1, :], turn_s[turn : turn + 1, :]
                cs.append(c * near_c - s * near_s)
                ss.append(s * near_c + c * near_s)
            place = slice(256 * j + 8 * r, 256 * j + 8 * r + 16)
            cos_k_ref[place, :] = jnp.concatenate(cs, axis=0).astype(BF16)
            sin_k_ref[place, :] = jnp.concatenate(ss, axis=0).astype(BF16)
    for f in range(32):
        c, s = base_c[f : f + 1, :], base_s[f : f + 1, :]
        first = 512 * (f % 2) + 32 * (f // 2)
        cos_y_ref[first : first + 32, :] = (c * turn_c - s * turn_s).astype(BF16)
        sin_y_ref[first : first + 32, :] = (s * turn_c + c * turn_s).astype(BF16)


def image_kernel(
    src_ref,
    info_ref,
    in_ref,
    target_ref,
    cos_k_ref,
    sin_k_ref,
    cos_ref,
    sin_ref,
    out_ref,
    info_out_ref,
    lhs_ref,
    grad_ref,
    flat_ref,
):
    step = pl.program_id(0)

    @pl.when(step == 0)
    def _():
        info_out_ref[...] = info_ref[...]
        for s in range(16):
            turned = in_ref[256 * s : 256 * s + 256, :].T
            for y in range(2):
                for j in range(4):
                    lhs_ref[32 * s + 16 * y : 32 * s + 16 * y + 16, 256 * j : 256 * j + 256] = turned[
                        64 * y + 16 * j : 64 * y + 16 * j + 16
                    ]

    @pl.when(step < STEPS)
    def _():
        by_cos = dot_nn(lhs_ref[...], cos_k_ref[...])
        by_sin = dot_nn(lhs_ref[...], sin_k_ref[...])

        cols = pl.ds(pl.multiple_of(step * CHUNK, CHUNK), CHUNK)

        def field(s, y):
            at = 32 * s + 16 * y
            re = by_cos[at : at + 8] - by_sin[at + 8 : at + 16]
            im = by_sin[at : at + 8] + by_cos[at + 8 : at + 16]
            return re, im

        for y in range(2):
            power = jnp.zeros((8, CHUNK), F32)
            for s in range(16):
                re, im = field(s, y)
                power += re * re + im * im
            intensity = jnp.sum(power, axis=0, keepdims=True) * (1.0 / 128.0)
            mismatch = intensity - target_ref[pl.ds(2 * src_ref[0] + y, 1), :]
            factor = 2.0 * mismatch
            for s in range(0, 16, 2):
                grads_re, grads_im = [], []
                for one in (s, s + 1):
                    re, im = field(one, y)
                    grads_re.append(factor * re)
                    grads_im.append(factor * im)
                at = 256 * y + 8 * s
                grad_ref[at : at + 16, cols] = jnp.concatenate(grads_re, axis=0).astype(BF16)
                grad_ref[at + 128 : at + 144, cols] = jnp.concatenate(grads_im, axis=0).astype(BF16)

    @pl.when(step >= STEPS)
    def _():
        by_cos = dot_nt(cos_ref[...], grad_ref[...])
        by_sin = dot_nt(sin_ref[...], grad_ref[...])
        for y in range(2):
            re, im = slice(256 * y, 256 * y + 128), slice(256 * y + 128, 256 * y + 256)
            flat_ref[pl.ds(2 * y, WIDE, stride=4), :] = by_cos[:, re] + by_sin[:, im]
            flat_ref[pl.ds(2 * y + 1, WIDE, stride=4), :] = by_cos[:, im] - by_sin[:, re]
        for r in range(16):
            for s in range(16):
                first_row = 8 * (16 * r + s)
                out_ref[s, r] = flat_ref[first_row : first_row + 8, :].astype(BF16)


def gradient_kernel(place_ref, src_ref, near_ref, far_ref, in_ref, cos_ref, sin_ref, out_ref, lhs_ref, flat_ref, sums_ref):
    step = pl.program_id(0)

    @pl.when(step == 0)
    def _():
        for first in range(0, 4096, 512):
            flat_ref[first : first + 512, :] = in_ref[first : first + 512, :].astype(F32)
        for k in range(2):
            for y in range(2):
                for c in range(2):
                    part = flat_ref[pl.ds(4 * k + 2 * y + c, 512, stride=8), :]
                    lhs_ref[128 * (2 * c + k) : 128 * (2 * c + k) + 128, 512 * y : 512 * y + 512] = part.astype(BF16).T

    by_cos = dot_nn(lhs_ref[...], cos_ref[...])
    by_sin = dot_nn(lhs_ref[...], sin_ref[...])
    gaps = [jnp.bitwise_xor(src_ref[0], s) for s in range(16)]
    info = jnp.concatenate([jnp.where(gap % 2 == 0, near_ref[gap // 2], far_ref[gap // 2]) for gap in gaps], axis=0)
    root, centre_row, centre_col = info[:, 0:1], info[:, 1:2], info[:, 2:3]
    first_col = (step * CHUNK).astype(F32)
    col_gap = lax.broadcasted_iota(jnp.int32, (LANES, CHUNK), 1).astype(F32) + (first_col - centre_col)
    col_gap = col_gap * col_gap
    for k in range(2):
        row_gap = (place_ref[0] + k).astype(F32) - centre_row
        keep = row_gap * row_gap + col_gap <= float(RAD * RAD)
        factor = jnp.where(keep, root, 0.0)
        re, im = slice(128 * k, 128 * k + 128), slice(256 + 128 * k, 256 + 128 * k + 128)
        terms = (by_cos[re] + by_sin[im], by_cos[im] - by_sin[re])
        for c in range(2):
            total = jnp.sum(factor * terms[c], axis=0, keepdims=True)
            for side in range(2):
                sums_ref[pl.ds(16 * k + 8 * c + 2 * step + side, 1), :] = total[:, side * LANES : (side + 1) * LANES]

    @pl.when(step == STEPS - 1)
    def _():
        for i in range(16):
            out_ref[i] = sums_ref[...].astype(BF16)


def unpack_kernel(in_ref, re_ref, im_ref, flat_ref):
    flat_ref[...] = in_ref[...].astype(F32)
    for c, ref in enumerate((re_ref, im_ref)):
        for tile in range(8):
            ref[:, tile * LANES : (tile + 1) * LANES] = flat_ref[pl.ds(8 * c + tile, 32, stride=16), :]


def exchange(value, axis):
    return lax.all_to_all(value, axis, split_axis=0, concat_axis=0, tiled=True)


def gather_info(info, bits):
    for bit in bits:
        info = jnp.concatenate([info, lax.ppermute(info, "src", [(i, i ^ bit) for i in range(16)])], axis=0)
    return info


def compute(spec_re, spec_im, target, weights, cent_row, cent_col):
    rows, band = spec_re.shape
    everyone = ("src", "row")
    row = lax.axis_index("row").astype(jnp.int32).reshape(1)
    src = lax.axis_index("src").astype(jnp.int32).reshape(1)
    trig = trig_rows(band)
    table = jax.ShapeDtypeStruct((band, band), BF16)
    parts = jax.ShapeDtypeStruct((16, 32, 8, LANES), BF16)
    col_block = pl.BlockSpec((band, CHUNK), lambda n: (0, n))
    scalars = (weights, cent_row, cent_col)

    column_parts, info = pl.pallas_call(
        spectrum_kernel,
        grid=(2,),
        in_specs=[SCALARS, SCALARS, SCALARS, SCALARS, WHOLE, WHOLE, WHOLE],
        out_specs=[pl.BlockSpec((16, 16, 8, LANES), lambda n: (0, n, 0, 0)), WHOLE],
        out_shape=[parts, jax.ShapeDtypeStruct((1, 8, LANES), F32)],
        scratch_shapes=[
            pltpu.VMEM((512, 2 * band), BF16),
            pltpu.VMEM((WIDE, 2 * band), BF16),
            pltpu.VMEM((4 * WIDE, LANES), F32),
        ],
        name="spectrum",
    )(row, *scalars, trig, spec_re, spec_im)
    cosine, sine, cos_k, sin_k, cos_y, sin_y = pl.pallas_call(
        tables_kernel,
        grid=(STEPS,),
        in_specs=[
            pl.BlockSpec((48, CHUNK), lambda n: (0, n)),
            pl.BlockSpec(memory_space=pl.ANY),
        ],
        out_specs=[col_block] * 6,
        out_shape=[table] * 6,
        cost_estimate=pl.CostEstimate(flops=18 * band * band, bytes_accessed=12 * band * band, transcendentals=0),
        name="tables",
    )(trig, column_parts)
    some_info = gather_info(info, (2, 4))
    cosine, sine, cos_k, sin_k, cos_y, sin_y = (
        pltpu.with_memory_space_constraint(one, pltpu.HBM) for one in (cosine, sine, cos_k, sin_k, cos_y, sin_y)
    )
    columns = exchange(column_parts.reshape(512, 8, LANES), everyone).reshape(4096, LANES)
    adjoint_parts, some_info = pl.pallas_call(
        image_kernel,
        grid=(STEPS + 2,),
        in_specs=[
            SCALARS,
            WHOLE,
            WHOLE,
            pl.BlockSpec((rows, CHUNK), lambda n: (0, jnp.minimum(n, STEPS - 1))),
            pl.BlockSpec((band, CHUNK), lambda n: (0, jnp.minimum(n, STEPS - 1))),
            pl.BlockSpec((band, CHUNK), lambda n: (0, jnp.minimum(n, STEPS - 1))),
            pl.BlockSpec((WIDE, band), lambda n: (jnp.maximum(n - STEPS, 0), 0)),
            pl.BlockSpec((WIDE, band), lambda n: (jnp.maximum(n - STEPS, 0), 0)),
        ],
        out_specs=[pl.BlockSpec((16, 16, 8, LANES), lambda n: (0, jnp.maximum(n - STEPS, 0), 0, 0)), WHOLE],
        out_shape=[parts, jax.ShapeDtypeStruct((4, 8, LANES), F32)],
        scratch_shapes=[
            pltpu.VMEM((512, band), BF16),
            pltpu.VMEM((512, band), BF16),
            pltpu.VMEM((4 * WIDE, LANES), F32),
        ],
        compiler_params=pltpu.CompilerParams(vmem_limit_bytes=40 * 2**20),
        name="image",
    )(src, some_info, columns, target, cos_k, sin_k, cosine, sine)
    adjoint = exchange(adjoint_parts.reshape(512, 8, LANES), everyone).reshape(4096, LANES)
    near_info = gather_info(some_info, (8,))
    far_info = lax.ppermute(near_info, "src", [(i, i ^ 1) for i in range(16)])
    gradient = pl.pallas_call(
        gradient_kernel,
        grid=(STEPS,),
        in_specs=[SCALARS, SCALARS, WHOLE, WHOLE, WHOLE, col_block, col_block],
        out_specs=WHOLE,
        out_shape=jax.ShapeDtypeStruct((16, 32, LANES), BF16),
        scratch_shapes=[
            pltpu.VMEM((512, band), BF16),
            pltpu.VMEM((4096, LANES), F32),
            pltpu.VMEM((32, LANES), F32),
        ],
        compiler_params=pltpu.CompilerParams(vmem_limit_bytes=40 * 2**20),
        name="gradient",
    )(row * rows + 2 * src, src, near_info, far_info, adjoint, cos_y, sin_y)
    gradient = exchange(gradient, "src").reshape(512, LANES)
    out = jax.ShapeDtypeStruct((rows, band), F32)
    return tuple(
        pl.pallas_call(
            unpack_kernel, out_shape=[out, out], scratch_shapes=[pltpu.VMEM((512, LANES), F32)], name="unpack"
        )(gradient)
    )


def solution(mesh):
    return jax.shard_map(
        compute,
        mesh=mesh,
        in_specs=(P("row", None), P("row", None), P("row", None), P("src"), P("src"), P("src")),
        out_specs=(P("row", None), P("row", None)),
        check_vma=False,
    )
```

```python
import math

import jax
import jax.numpy as jnp
from jax import lax
from jax.experimental import pallas as pl
from jax.experimental.pallas import tpu as pltpu
from jax.sharding import PartitionSpec as P


RAD = 128
F32 = jnp.float32
BF16 = jnp.bfloat16
CHUNK = 256
WIDE = 512
LANES = 128
STEPS = 4

WHOLE = pl.BlockSpec(memory_space=pltpu.VMEM)
SCALARS = pl.BlockSpec(memory_space=pltpu.SMEM)


def trig_rows(band):
    index = jnp.arange(24, dtype=jnp.int32)
    rows = jnp.where(index < 8, index, 128 * (index - 8))
    rows = jnp.where(index < 16, rows, jnp.where(index < 20, 8 * (index - 16), 32 * (index - 20)))
    phase = rows[:, None] * jnp.arange(band, dtype=jnp.int32)[None, :]
    both = jnp.concatenate([phase, phase + (band - band // 4)], axis=0) % band
    return jnp.cos(both.astype(F32) * (2.0 * math.pi / band))


def rotate(one, other):
    return one[0] * other[0] - one[1] * other[1], one[1] * other[0] + one[0] * other[1]


def pick(trig, first, count=1):
    return trig[first : first + count, :], trig[24 + first : 24 + first + count, :]


def base_rows(trig, scale):
    fine = tuple(part * scale for part in pick(trig, 0, 8))
    blocks = [rotate(pick(trig, 16 + b), fine) for b in range(4)]
    return tuple(jnp.concatenate([block[i] for block in blocks], axis=0) for i in range(2))


def info_tile(w_ref, cr_ref, cc_ref):
    shape = (8, LANES)
    sublane = lax.broadcasted_iota(jnp.int32, shape, 0)
    lane = lax.broadcasted_iota(jnp.int32, shape, 1)
    tile = jnp.zeros(shape, F32)
    for p in range(8):
        centre = jnp.where(lane == 1, cr_ref[p].astype(F32), cc_ref[p].astype(F32))
        tile = jnp.where(sublane == p, jnp.where(lane == 0, jnp.sqrt(jnp.full(shape, w_ref[p], F32)), centre), tile)
    return tile


def dot_nt(left, right):
    return lax.dot_general(left, right, (((1,), (1,)), ((), ())), preferred_element_type=F32)


def dot_nn(left, right):
    return jnp.dot(left, right, preferred_element_type=F32)


def spectrum_kernel(row_ref, w_ref, cr_ref, cc_ref, trig_ref, re_ref, im_ref, out_ref, info_ref, lhs_ref, table_ref, flat_ref):
    step = pl.program_id(0)
    rows, band = re_ref.shape

    @pl.when(step == 0)
    def _():
        spec_re = re_ref[...].astype(F32)
        spec_im = im_ref[...].astype(F32)
        info = info_tile(w_ref, cr_ref, cc_ref)
        info_ref[0] = info
        centre_row, centre_col = info[:, 1:2], info[:, 2:3]
        col_gap = lax.broadcasted_iota(jnp.int32, (8, band), 1).astype(F32) - centre_col
        col_gap = col_gap * col_gap
        first = (row_ref[0] * rows).astype(F32)
        for k in range(rows):
            row_gap = first + float(k) - centre_row
            keep = row_gap * row_gap + col_gap <= float(RAD * RAD)
            part_re = jnp.where(keep, spec_re[k : k + 1, :], 0.0)
            part_im = jnp.where(keep, spec_im[k : k + 1, :], 0.0)
            place = slice(16 * k, 16 * k + 16)
            lhs_ref[place, :band] = jnp.concatenate([part_re, part_im], axis=0).astype(BF16)
            lhs_ref[place, band:] = jnp.concatenate([-part_im, part_re], axis=0).astype(BF16)

    base = base_rows(trig_ref, 1.0 / math.sqrt(band))
    for a in range(4):
        coarse = tuple(trig_ref[pl.ds(first + 4 * step + a, 1), :] for first in (8, 32))
        for d in range(4):
            cos, sin = rotate(rotate(coarse, pick(trig_ref, 20 + d)), base)
            place = slice(128 * a + 32 * d, 128 * a + 32 * d + 32)
            table_ref[place, :band] = cos.astype(BF16)
            table_ref[place, band:] = sin.astype(BF16)
    product = dot_nt(table_ref[...], lhs_ref[...])
    point = lax.broadcasted_iota(jnp.int32, (8, LANES), 1) % 8
    root = jnp.zeros((8, LANES), F32)
    for p in range(8):
        root = jnp.where(point == p, w_ref[p], root)
    root = jnp.sqrt(root)[0:1, :]
    for t in range(4):
        flat_ref[pl.ds(t, WIDE, stride=4), :] = product[:, t * LANES : (t + 1) * LANES] * root
    low_row = lax.broadcasted_iota(jnp.int32, (8, LANES), 0) < 4
    low_lane = lax.broadcasted_iota(jnp.int32, (8, LANES), 1) < 64
    stay = low_row == low_lane
    for r in range(16):
        for s in range(16):
            first_row = 8 * (16 * r + s)
            tile = flat_ref[first_row : first_row + 8, :]
            moved = pltpu.roll(pltpu.roll(tile, 4, 0), 64, 1)
            out_ref[s, r] = jnp.where(stay, tile, moved).astype(BF16)


def tables_kernel(
    trig_ref, _, cos_ref, sin_ref, cos_k_ref, sin_k_ref, cos_y_ref, sin_y_ref
):
    base_c, base_s = base_rows(trig_ref, 1.0 / math.sqrt(4 * trig_ref.shape[1]))
    turns = [rotate(pick(trig_ref, 8 + a), pick(trig_ref, 20 + d)) for a in range(8) for d in range(4)]
    turn_c, turn_s = (jnp.concatenate([turn[i] for turn in turns], axis=0) for i in range(2))
    for r in range(32):
        cos, sin = rotate(turns[r], (base_c, base_s))
        cos_ref[32 * r : 32 * r + 32, :] = cos.astype(BF16)
        sin_ref[32 * r : 32 * r + 32, :] = sin.astype(BF16)
    for j in range(4):
        order = [j + 8 * (i % 4) + 4 * (i // 4) for i in range(8)]
        near_c = jnp.concatenate([base_c[f : f + 1, :] for f in order], axis=0)
        near_s = jnp.concatenate([base_s[f : f + 1, :] for f in order], axis=0)
        for r in range(0, 32, 2):
            cs, ss = [], []
            for turn in (r, r + 1):
                c, s = turn_c[turn : turn + 1, :], turn_s[turn : turn + 1, :]
                cs.append(c * near_c - s * near_s)
                ss.append(s * near_c + c * near_s)
            place = slice(256 * j + 8 * r, 256 * j + 8 * r + 16)
            cos_k_ref[place, :] = jnp.concatenate(cs, axis=0).astype(BF16)
            sin_k_ref[place, :] = jnp.concatenate(ss, axis=0).astype(BF16)
    for f in range(32):
        c, s = base_c[f : f + 1, :], base_s[f : f + 1, :]
        first = 512 * (f % 2) + 32 * (f // 2)
        cos_y_ref[first : first + 32, :] = (c * turn_c - s * turn_s).astype(BF16)
        sin_y_ref[first : first + 32, :] = (s * turn_c + c * turn_s).astype(BF16)


def image_kernel(
    src_ref,
    in_ref,
    target_ref,
    cos_k_ref,
    sin_k_ref,
    cos_ref,
    sin_ref,
    out_ref,
    lhs_ref,
    grad_ref,
    flat_ref,
):
    step = pl.program_id(0)

    @pl.when(step == 0)
    def _():
        for s in range(16):
            turned = in_ref[256 * s : 256 * s + 256, :].T
            for y in range(2):
                for j in range(4):
                    lhs_ref[32 * s + 16 * y : 32 * s + 16 * y + 16, 256 * j : 256 * j + 256] = turned[
                        64 * y + 16 * j : 64 * y + 16 * j + 16
                    ]

    @pl.when(step < STEPS)
    def _():
        by_cos = dot_nn(lhs_ref[...], cos_k_ref[...])
        by_sin = dot_nn(lhs_ref[...], sin_k_ref[...])

        cols = pl.ds(pl.multiple_of(step * CHUNK, CHUNK), CHUNK)

        def field(s, y):
            at = 32 * s + 16 * y
            re = by_cos[at : at + 8] - by_sin[at + 8 : at + 16]
            im = by_sin[at : at + 8] + by_cos[at + 8 : at + 16]
            return re, im

        for y in range(2):
            power = jnp.zeros((8, CHUNK), F32)
            for s in range(16):
                re, im = field(s, y)
                power += re * re + im * im
            intensity = jnp.sum(power, axis=0, keepdims=True) * (1.0 / 128.0)
            mismatch = intensity - target_ref[pl.ds(2 * src_ref[0] + y, 1), :]
            factor = 2.0 * mismatch
            for s in range(0, 16, 2):
                grads_re, grads_im = [], []
                for one in (s, s + 1):
                    re, im = field(one, y)
                    grads_re.append(factor * re)
                    grads_im.append(factor * im)
                at = 256 * y + 8 * s
                grad_ref[at : at + 16, cols] = jnp.concatenate(grads_re, axis=0).astype(BF16)
                grad_ref[at + 128 : at + 144, cols] = jnp.concatenate(grads_im, axis=0).astype(BF16)

    @pl.when(step >= STEPS)
    def _():
        by_cos = dot_nt(cos_ref[...], grad_ref[...])
        by_sin = dot_nt(sin_ref[...], grad_ref[...])
        for y in range(2):
            re, im = slice(256 * y, 256 * y + 128), slice(256 * y + 128, 256 * y + 256)
            flat_ref[pl.ds(2 * y, WIDE, stride=4), :] = by_cos[:, re] + by_sin[:, im]
            flat_ref[pl.ds(2 * y + 1, WIDE, stride=4), :] = by_cos[:, im] - by_sin[:, re]
        for r in range(16):
            for s in range(16):
                first_row = 8 * (16 * r + s)
                out_ref[s, r] = flat_ref[first_row : first_row + 8, :].astype(BF16)


def gradient_kernel(place_ref, src_ref, near_ref, far_ref, in_ref, cos_ref, sin_ref, out_ref, lhs_ref, flat_ref, sums_ref):
    step = pl.program_id(0)

    @pl.when(step == 0)
    def _():
        for first in range(0, 4096, 512):
            flat_ref[first : first + 512, :] = in_ref[first : first + 512, :].astype(F32)
        for k in range(2):
            for y in range(2):
                for c in range(2):
                    part = flat_ref[pl.ds(4 * k + 2 * y + c, 512, stride=8), :]
                    lhs_ref[128 * (2 * c + k) : 128 * (2 * c + k) + 128, 512 * y : 512 * y + 512] = part.astype(BF16).T

    by_cos = dot_nn(lhs_ref[...], cos_ref[...])
    by_sin = dot_nn(lhs_ref[...], sin_ref[...])

    def place(gap):
        return gap % 8

    gaps = [jnp.bitwise_xor(src_ref[0], s) for s in range(16)]
    info = jnp.concatenate([jnp.where(gap < 8, near_ref[place(gap)], far_ref[place(gap)]) for gap in gaps], axis=0)
    root, centre_row, centre_col = info[:, 0:1], info[:, 1:2], info[:, 2:3]
    first_col = (step * CHUNK).astype(F32)
    col_gap = lax.broadcasted_iota(jnp.int32, (LANES, CHUNK), 1).astype(F32) + (first_col - centre_col)
    col_gap = col_gap * col_gap
    for k in range(2):
        row_gap = (place_ref[0] + k).astype(F32) - centre_row
        keep = row_gap * row_gap + col_gap <= float(RAD * RAD)
        factor = jnp.where(keep, root, 0.0)
        re, im = slice(128 * k, 128 * k + 128), slice(256 + 128 * k, 256 + 128 * k + 128)
        terms = (by_cos[re] + by_sin[im], by_cos[im] - by_sin[re])
        for c in range(2):
            total = jnp.sum(factor * terms[c], axis=0, keepdims=True)
            for side in range(2):
                sums_ref[pl.ds(16 * k + 8 * c + 2 * step + side, 1), :] = total[:, side * LANES : (side + 1) * LANES]

    @pl.when(step == STEPS - 1)
    def _():
        for i in range(16):
            out_ref[i] = sums_ref[...].astype(BF16)


def unpack_kernel(in_ref, re_ref, im_ref, flat_ref):
    flat_ref[...] = in_ref[...].astype(F32)
    for c, ref in enumerate((re_ref, im_ref)):
        for tile in range(8):
            ref[:, tile * LANES : (tile + 1) * LANES] = flat_ref[pl.ds(8 * c + tile, 32, stride=16), :]


def exchange(value, axis):
    return lax.all_to_all(value, axis, split_axis=0, concat_axis=0, tiled=True)


def gather_info(info, bits):
    for bit in bits:
        info = jnp.concatenate([info, lax.ppermute(info, "src", [(i, i ^ bit) for i in range(16)])], axis=0)
    return info


def compute(spec_re, spec_im, target, weights, cent_row, cent_col):
    rows, band = spec_re.shape
    everyone = ("src", "row")
    row = lax.axis_index("row").astype(jnp.int32).reshape(1)
    src = lax.axis_index("src").astype(jnp.int32).reshape(1)
    trig = trig_rows(band)
    table = jax.ShapeDtypeStruct((band, band), BF16)
    parts = jax.ShapeDtypeStruct((16, 32, 8, LANES), BF16)
    col_block = pl.BlockSpec((band, CHUNK), lambda n: (0, n))
    scalars = (weights, cent_row, cent_col)

    column_parts, info = pl.pallas_call(
        spectrum_kernel,
        grid=(2,),
        in_specs=[SCALARS, SCALARS, SCALARS, SCALARS, WHOLE, WHOLE, WHOLE],
        out_specs=[pl.BlockSpec((16, 16, 8, LANES), lambda n: (0, n, 0, 0)), WHOLE],
        out_shape=[parts, jax.ShapeDtypeStruct((1, 8, LANES), F32)],
        scratch_shapes=[
            pltpu.VMEM((512, 2 * band), BF16),
            pltpu.VMEM((WIDE, 2 * band), BF16),
            pltpu.VMEM((4 * WIDE, LANES), F32),
        ],
        name="spectrum",
    )(row, *scalars, trig, spec_re, spec_im)
    cosine, sine, cos_k, sin_k, cos_y, sin_y = pl.pallas_call(
        tables_kernel,
        grid=(STEPS,),
        in_specs=[
            pl.BlockSpec((48, CHUNK), lambda n: (0, n)),
            pl.BlockSpec(memory_space=pl.ANY),
        ],
        out_specs=[col_block] * 6,
        out_shape=[table] * 6,
        cost_estimate=pl.CostEstimate(flops=18 * band * band, bytes_accessed=12 * band * band, transcendentals=0),
        name="tables",
    )(trig, column_parts)
    near_info = gather_info(info, (1, 2, 4))
    cosine, sine, cos_k, sin_k, cos_y, sin_y = (
        pltpu.with_memory_space_constraint(one, pltpu.HBM) for one in (cosine, sine, cos_k, sin_k, cos_y, sin_y)
    )
    columns = exchange(column_parts.reshape(512, 8, LANES), everyone).reshape(4096, LANES)
    adjoint_parts = pl.pallas_call(
        image_kernel,
        grid=(STEPS + 2,),
        in_specs=[
            SCALARS,
            WHOLE,
            pl.BlockSpec((rows, CHUNK), lambda n: (0, jnp.minimum(n, STEPS - 1))),
            pl.BlockSpec((band, CHUNK), lambda n: (0, jnp.minimum(n, STEPS - 1))),
            pl.BlockSpec((band, CHUNK), lambda n: (0, jnp.minimum(n, STEPS - 1))),
            pl.BlockSpec((WIDE, band), lambda n: (jnp.maximum(n - STEPS, 0), 0)),
            pl.BlockSpec((WIDE, band), lambda n: (jnp.maximum(n - STEPS, 0), 0)),
        ],
        out_specs=pl.BlockSpec((16, 16, 8, LANES), lambda n: (0, jnp.maximum(n - STEPS, 0), 0, 0)),
        out_shape=parts,
        scratch_shapes=[
            pltpu.VMEM((512, band), BF16),
            pltpu.VMEM((512, band), BF16),
            pltpu.VMEM((4 * WIDE, LANES), F32),
        ],
        compiler_params=pltpu.CompilerParams(vmem_limit_bytes=40 * 2**20),
        name="image",
    )(src, columns, target, cos_k, sin_k, cosine, sine)
    adjoint = exchange(adjoint_parts.reshape(512, 8, LANES), everyone).reshape(4096, LANES)
    far_info = lax.ppermute(near_info, "src", [(i, i ^ 8) for i in range(16)])
    gradient = pl.pallas_call(
        gradient_kernel,
        grid=(STEPS,),
        in_specs=[SCALARS, SCALARS, WHOLE, WHOLE, WHOLE, col_block, col_block],
        out_specs=WHOLE,
        out_shape=jax.ShapeDtypeStruct((16, 32, LANES), BF16),
        scratch_shapes=[
            pltpu.VMEM((512, band), BF16),
            pltpu.VMEM((4096, LANES), F32),
            pltpu.VMEM((32, LANES), F32),
        ],
        compiler_params=pltpu.CompilerParams(vmem_limit_bytes=40 * 2**20),
        name="gradient",
    )(row * rows + 2 * src, src, near_info, far_info, adjoint, cos_y, sin_y)
    gradient = exchange(gradient, "src").reshape(512, LANES)
    out = jax.ShapeDtypeStruct((rows, band), F32)
    return tuple(
        pl.pallas_call(
            unpack_kernel, out_shape=[out, out], scratch_shapes=[pltpu.VMEM((512, LANES), F32)], name="unpack"
        )(gradient)
    )


def solution(mesh):
    return jax.shard_map(
        compute,
        mesh=mesh,
        in_specs=(P("row", None), P("row", None), P("row", None), P("src"), P("src"), P("src")),
        out_specs=(P("row", None), P("row", None)),
        check_vma=False,
    )
```
